32 devices in a mesh: level: 2 (over y), sub: 16 (over z, x, core).
Axes of the slice: x: 2, y: 2, z: 4, core: 2. Of those that a mesh axis runs over, the one named last changes fastest.
Arguments:
- factor_inv: float32 [2, 16, 256, 256], P('level', 'sub'), may hold values from -0.0625 to 1.4, as said below
- update_blocks: float32 [2, 16, 4, 128, 256], P('level', 'sub'), may hold values from -0.1875 to 0.1875
- update_rows: int32 [2, 16, 4], P('level', 'sub'), may hold values from 0 to 3, each once within a row
- right_side: float32 [2, 16, 256, 512], P('level', 'sub'), may hold values from -4000 to 4000
Outputs:
- solution: float32 [2, 16, 256, 512], P('level', 'sub')
The draws below stay inside these ranges and needn't reach their ends.
Inputs may be any that keep to these rules, and one draw needn't show every extreme that they name: `update_rows`: each supernode's 4 update blocks name the 4 target row blocks once each; values below 2 are row blocks of the parent supernode in the same subtree, the others those of the parent supernode in the next subtree (the last subtree's next is the first). `factor_inv`: each 256 x 256 block is lower triangular, with diagonal entries between 0.7 and 1.4.
All inputs are finite; a program needn't handle non-finite values.
Results may differ from the reference program's by a relative error of at most 0.00014.
Values sent between devices are 32-bit elements; how exact they have to be, the bound alone decides.
A program may use at most 64 MiB of HBM per device.

```python
import math
import jax
import jax.numpy as jnp
from jax import lax

W = 256
BLK = 128
R = 512
NRB = 2
K = 4
N_LEVEL = 2
N_SUB = 16


def draw_factor_inv(key, part):
    full_shape = (N_LEVEL, N_SUB, W, W)
    key_one, key_two = jax.random.split(key, 2)
    row_index = lax.broadcasted_iota(jnp.int32, full_shape, 2)
    col_index = lax.broadcasted_iota(jnp.int32, full_shape, 3)
    off_diag = jnp.clip(0.6 * jax.random.normal(key_one, full_shape, jnp.float32), -1.0, 1.0)
    diag_vals = jnp.exp(jax.random.uniform(key_two, full_shape, jnp.float32, math.log(0.7), math.log(1.4)))
    off_diag = off_diag / math.sqrt(W)
    return jnp.where(row_index > col_index, off_diag, jnp.where(row_index == col_index, diag_vals, 0.0)).astype(jnp.float32)


def draw_right_side(key, part):
    full_shape = (N_LEVEL, N_SUB, W, R)
    key_one, key_two, key_three = jax.random.split(key, 3)
    position = (lax.broadcasted_iota(jnp.float32, full_shape, 0) * N_SUB + lax.broadcasted_iota(jnp.float32, full_shape, 1)) / max(N_LEVEL * N_SUB - 1, 1)
    rise_factor = 1.0 + 2.0 * position
    row_scale = jnp.exp(jax.random.uniform(key_two, (N_LEVEL, N_SUB, W, 1), jnp.float32, 0.0, math.log(10.0)))
    col_scale = jnp.exp(jax.random.uniform(key_three, (1, 1, 1, R), jnp.float32, 0.0, math.log(10.0)))
    base_vals = jnp.clip(jax.random.normal(key_one, full_shape, jnp.float32), -4.0, 4.0)
    return (base_vals * rise_factor * row_scale * col_scale).astype(jnp.float32)


def shard_levels(stream_key, extent, shards, low, top_value):
    level, own = 1.0, jax.random.fold_in(stream_key, 6)
    for dim, parts in shards:
        draws = jnp.exp(jax.random.uniform(jax.random.fold_in(own, dim), (parts,), jnp.float32, low / len(shards), top_value / len(shards)))
        level = level * jnp.repeat(draws, extent[dim] // parts).reshape([-1 if axis == dim else 1 for axis in range(len(extent))])
    return level


def noise(rng, extent, width, most, cuts=(), held_as=jnp.bfloat16):
    array = jax.random.normal(rng, extent, jnp.float32) * width
    if len(cuts) > 0:
        array = shard_levels(rng, extent, cuts, -0.22, 0.18) * array
    return jnp.clip(array, min=-most, max=most).astype(held_as)


def setup_inputs(seed: int = 0) -> dict:
    keys = jax.random.split(jax.random.key(seed), 5)
    return {
        "factor_inv": draw_factor_inv(jax.random.fold_in(keys[4], 71), 0),
        "update_blocks": noise(keys[1], (N_LEVEL, N_SUB, K, BLK, W), (4 * W) ** -0.5, 0.1875, ((0, 2), (1, 16)), jnp.float32),
        "update_rows": jax.vmap(lambda own: jax.random.permutation(own, K))(jax.random.split(keys[2], N_LEVEL * N_SUB)).reshape((N_LEVEL, N_SUB, K)).astype(jnp.int32),
        "right_side": draw_right_side(jax.random.fold_in(keys[4], 71), 0),
    }


FULL_PRECISION = lax.Precision.HIGHEST

def reference(factor_inv, update_blocks, update_rows, right_side):
    norm_total = lax.optimization_barrier(jnp.sum(right_side * right_side, axis=(0, 1, 2)))
    col_scale = jnp.sqrt(norm_total / (N_LEVEL * N_SUB * W) + 1e-06)
    onehot = (update_rows[:, :, :, None] == jnp.arange(K, dtype=jnp.int32)[None, None, None, :]).astype(jnp.float32)
    incoming = jnp.zeros((N_SUB, W, R), jnp.float32)
    forward = []
    for level_no in range(N_LEVEL):
        forward_val = jnp.einsum('sij,sjc->sic', factor_inv[level_no], right_side[level_no] - incoming, precision=FULL_PRECISION)
        forward.append(forward_val)
        if level_no + 1 < N_LEVEL:
            pieces = jnp.einsum('skbj,sjc->skbc', update_blocks[level_no], forward_val, precision=FULL_PRECISION)
            slot_sums = jnp.einsum('skd,skbc->sdbc', onehot[level_no], pieces, precision=FULL_PRECISION)
            incoming = (slot_sums[:, :NRB] + jnp.roll(slot_sums[:, NRB:], 1, axis=0)).reshape(N_SUB, W, R)
    result_levels = [forward[0]] * N_LEVEL
    parent_x = jnp.zeros((N_SUB, W, R), jnp.float32)
    for level_no in reversed(range(N_LEVEL)):
        rhs_now = forward[level_no]
        if level_no + 1 < N_LEVEL:
            own_blocks = parent_x.reshape(N_SUB, NRB, BLK, R)
            paired = jnp.concatenate([own_blocks, jnp.roll(own_blocks, -1, axis=0)], axis=1)
            picked = jnp.einsum('skd,sdbc->skbc', onehot[level_no], paired, precision=FULL_PRECISION)
            rhs_now = rhs_now - jnp.einsum('skbj,skbc->sjc', update_blocks[level_no], picked, precision=FULL_PRECISION)
        parent_x = jnp.einsum('sji,sjc->sic', factor_inv[level_no], rhs_now, precision=FULL_PRECISION)
        result_levels[level_no] = parent_x
    return jnp.stack(result_levels) / col_scale
```

```python
import functools

import jax
import jax.numpy as jnp
from jax import lax
from jax.experimental import pallas as pl
from jax.experimental.pallas import tpu as pltpu
from jax.sharding import PartitionSpec as P

LANES = 128
MESH = pl.DeviceIdType.MESH


def halves(value):
    high = value.astype(jnp.bfloat16)
    low = (value - high.astype(jnp.float32)).astype(jnp.bfloat16)
    return high, low


def left_operand(matrix):
    high, low = halves(matrix)
    return jnp.concatenate([high, low, high], axis=1)


def right_operand(values):
    high, low = halves(values)
    return jnp.concatenate([high, high, low], axis=0)


def product(left, right):
    return jnp.dot(left, right, preferred_element_type=jnp.float32)


def kernel(
    levels,
    subs,
    rows_hbm,
    inverse_hbm,
    blocks_hbm,
    rhs_hbm,
    x_ref,
    rows,
    inverse,
    blocks,
    rhs,
    operands,
    spread_own,
    spread_next,
    turned_own,
    turned_next,
    gram,
    gram_top,
    base,
    own,
    next_out,
    next_in,
    up_in,
    own_in,
    beside_in,
    solved,
    top_corner,
    top_rows,
    top_rhs,
    part,
    pair_in,
    rise_in,
    gathered,
    hub_in,
    total_in,
    factor,
    load_sem,
    give_send,
    give_recv,
    next_send,
    next_recv,
    up_send,
    up_recv,
    down_send,
    down_recv,
    side_send,
    side_recv,
    sums_send,
    sums_recv,
    hub_send,
    hub_recv,
):
    level = lax.axis_index("level")
    sub = lax.axis_index("sub")
    chunks = rhs.shape[0]
    width = inverse.shape[0]
    half = width // 2
    slots = blocks.shape[0]
    hubs = subs // 2
    right = {"sub": lax.rem(sub + 1, subs)}
    left = {"sub": lax.rem(sub + subs - 1, subs)}
    above = {"level": level + 1}
    below = {"level": level - 1}
    others = [{"sub": lax.rem(sub + 2 * j, subs)} for j in range(1, hubs)]
    even = lax.rem(sub, 2) == 0
    odd = jnp.logical_not(even)
    is_top = level == levels - 1
    has_up = level < levels - 1
    is_host = jnp.logical_and(level == levels - 2, even)

    rows_load = pltpu.make_async_copy(rows_hbm, rows, load_sem.at[0])
    block_load = pltpu.make_async_copy(blocks_hbm, blocks, load_sem.at[1])
    inverse_load = pltpu.make_async_copy(inverse_hbm, inverse, load_sem.at[2])
    rhs_loads = [
        pltpu.make_async_copy(
            rhs_hbm.at[:, pl.ds(c * LANES, LANES)], rhs.at[c], load_sem.at[3 + c]
        )
        for c in range(chunks)
    ]

    barrier = pltpu.get_barrier_semaphore()

    def greet(device):
        pl.semaphore_signal(barrier, inc=1, device_id=device, device_id_type=MESH)

    @pl.when(has_up)
    def _():
        for device in (left, right, above):
            greet(device)
        rows_load.start()
        block_load.start()

    @pl.when(level > 0)
    def _():
        greet(below)

    @pl.when(jnp.logical_and(is_top, even))
    def _():
        greet(right)

    @pl.when(jnp.logical_and(is_top, odd))
    def _():
        greet(left)
        for device in others:
            greet(device)

    greetings = jnp.where(has_up, 3, jnp.where(even, 1, hubs)) + jnp.where(level > 0, 1, 0)

    inverse_load.start()
    for load in rhs_loads:
        load.start()

    def remote(source, target, send, recv, device):
        return pltpu.make_async_remote_copy(
            src_ref=source,
            dst_ref=target,
            send_sem=send,
            recv_sem=recv,
            device_id=device,
            device_id_type=MESH,
        )

    def chunk_copies(source, target, send, recv, device):
        return [
            remote(source.at[c], target.at[c], send.at[c], recv.at[c], device)
            for c in range(chunks)
        ]

    give_copy = [
        remote(
            inverse_hbm.at[pl.ds(0, half), pl.ds(0, half)],
            top_corner,
            give_send.at[0],
            give_recv.at[0],
            below,
        ),
        remote(
            inverse_hbm.at[pl.ds(half, half)], top_rows, give_send.at[1], give_recv.at[1], below
        ),
    ]
    for c in range(chunks):
        give_copy.append(
            remote(
                rhs_hbm.at[:, pl.ds(c * LANES, LANES)],
                top_rhs.at[c],
                give_send.at[2 + c],
                give_recv.at[2 + c],
                below,
            )
        )
    next_copy = chunk_copies(next_out, next_in, next_send, next_recv, right)
    up_copy = chunk_copies(own, up_in, up_send, up_recv, above)
    lift_copy = chunk_copies(own_in, solved, up_send, up_recv, above)
    down_copy = chunk_copies(solved, own_in, down_send, down_recv, below)
    side_copy = chunk_copies(own_in, beside_in, side_send, side_recv, left)
    pair_copy = remote(part, pair_in, sums_send.at[0], sums_recv.at[0], right)
    rise_copy = remote(gathered, rise_in, sums_send.at[1], sums_recv.at[1], above)
    fall_copy = remote(total_in, total_in, sums_send.at[2], sums_recv.at[2], below)
    mate_copy = remote(total_in, total_in, sums_send.at[3], sums_recv.at[3], left)
    hub_copy = [
        remote(gathered, hub_in.at[j], hub_send.at[j], hub_recv.at[j], others[j])
        for j in range(hubs - 1)
    ]

    def placed(slot):
        found = jnp.int32(0)
        for k in range(slots):
            found = jnp.where(rows[k] == slot, k, found)
        return blocks[found]

    def spread_matrix(first):
        picked = [placed(first + d) for d in range(slots // 2)]
        ordered = jnp.concatenate(picked, axis=0)
        return product(left_operand(ordered), right_operand(inverse[...]))

    def squared(matrix):
        return left_operand(product(left_operand(matrix.T), right_operand(matrix)))

    def make_part():
        for c in range(chunks):
            value = rhs[c]
            part[:, pl.ds(c * LANES, LANES)] = jnp.sum(value * value, axis=0, keepdims=True)

    def gather_pair():
        pair_copy.wait_recv()
        if levels > 2:

            @pl.when(level > 0)
            def _():
                rise_copy.wait_recv()

            gathered[...] = part[...] + pair_in[...] + jnp.where(level > 0, rise_in[...], 0.0)
        else:
            gathered[...] = part[...] + pair_in[...]

    def make_factor():
        factor[...] = 1.0 / jnp.sqrt(total_in[...] / (levels * subs * width) + 1e-06)

    def store(c, value):
        span = pl.ds(c * LANES, LANES)
        x_ref[:, span] = value * factor[:, span]

    @pl.when(jnp.logical_and(is_top, even))
    def _():
        pl.semaphore_wait(barrier, greetings)
        for copy in give_copy:
            copy.start()
        for load in rhs_loads:
            load.wait()
        make_part()
        pair_copy.start()
        inverse_load.wait()
        pair_copy.wait_send()
        for copy in give_copy:
            copy.wait_send()
        mate_copy.wait_recv()
        make_factor()
        for c in range(chunks):
            lift_copy[c].wait_recv()
            store(c, solved[c])

    @pl.when(jnp.logical_and(is_top, odd))
    def _():
        for load in rhs_loads:
            load.wait()
        make_part()
        inverse_load.wait()
        gram[...] = squared(inverse[...])
        pl.semaphore_wait(barrier, greetings)

        def solve(c):
            up_copy[c].wait_recv()
            solved[c] = product(gram[...], right_operand(rhs[c] - up_in[c]))
            down_copy[c].start()

        solve(0)
        pair_copy.wait_recv()
        rise_copy.wait_recv()
        gathered[...] = part[...] + pair_in[...] + rise_in[...]
        for copy in hub_copy:
            copy.start()
        for c in range(1, chunks - 1):
            solve(c)
        value = gathered[...]
        for j in range(hubs - 1):
            hub_copy[j].wait_recv()
            value = value + hub_in[j]
        total_in[...] = value
        fall_copy.start()
        mate_copy.start()
        solve(chunks - 1)
        make_factor()
        for c in range(chunks):
            store(c, solved[c])
        for copy in hub_copy + [fall_copy, mate_copy] + down_copy:
            copy.wait_send()

    def make_next():
        matrix = spread_matrix(slots // 2)
        spread_next[...] = left_operand(matrix)

    def make_own():
        matrix = spread_matrix(0)
        spread_own[...] = left_operand(matrix)

    def make_turned():
        for matrix, turned in ((spread_own, turned_own), (spread_next, turned_next)):
            for piece in range(3):
                span = pl.ds(piece * width, width)
                turned[:, span] = matrix[:, span].T

    def take(c):
        rhs_loads[c].wait()
        value = rhs[c]
        if levels > 2:

            @pl.when(level > 0)
            def _():
                up_copy[c].wait_recv()

            value = value - jnp.where(level > 0, up_in[c], 0.0)
        operands[c] = right_operand(value)

    def make_base():
        gram[...] = squared(inverse[...])
        for c in range(chunks):
            base[c] = product(gram[...], operands[c])

    def send_next(c):
        take(c)
        next_out[c] = product(spread_next[...], operands[c])
        if c == 0:
            pl.semaphore_wait(barrier, greetings)
        next_copy[c].start()

    def hand_down(c, value):
        if levels > 2:

            @pl.when(level > 0)
            def _():
                solved[c] = value
                down_copy[c].start()

    def await_down():
        if levels > 2:

            @pl.when(level > 0)
            def _():
                for c in range(chunks):
                    down_copy[c].wait_send()

    @pl.when(is_host)
    def _():
        rows_load.wait()
        block_load.wait()
        inverse_load.wait()
        make_next()
        for c in range(chunks):
            send_next(c)
        make_part()
        pair_copy.start()
        make_own()
        for c in range(chunks):
            own[c] = product(spread_own[...], operands[c])
        make_turned()
        make_base()
        give_copy[0].wait_recv()
        give_copy[1].wait_recv()
        corner = jnp.concatenate([top_corner[...], jnp.zeros((half, half), jnp.float32)], axis=1)
        gram_top[...] = squared(jnp.concatenate([corner, top_rows[...]], axis=0))
        for c in range(chunks):
            next_copy[c].wait_recv()
            give_copy[2 + c].wait_recv()
            operand = right_operand(top_rhs[c] - (own[c] + next_in[c]))
            value = product(gram_top[...], operand)
            own_in[c] = value
            lift_copy[c].start()
            side_copy[c].start()
            base[c] = base[c] - product(turned_own[...], right_operand(value))
        mate_copy.wait_recv()
        make_factor()
        for c in range(chunks):
            side_copy[c].wait_recv()
            value = base[c] - product(turned_next[...], right_operand(beside_in[c]))
            hand_down(c, value)
            store(c, value)
        for copy in next_copy + [pair_copy] + lift_copy + side_copy:
            copy.wait_send()
        await_down()

    def climb(leads):
        rows_load.wait()
        block_load.wait()
        inverse_load.wait()
        make_next()
        early = min(2, chunks)
        for c in range(early):
            send_next(c)
        make_own()
        for c in range(early):
            own[c] = product(spread_own[...], operands[c])
        for c in range(early):
            next_copy[c].wait_recv()
            own[c] = own[c] + next_in[c]
            up_copy[c].start()
        for c in range(early, chunks):
            send_next(c)
            own[c] = product(spread_own[...], operands[c])
        for c in range(early, chunks):
            next_copy[c].wait_recv()
            own[c] = own[c] + next_in[c]
            up_copy[c].start()
        make_part()
        if leads:
            gather_pair()
            rise_copy.start()
        else:
            pair_copy.start()
        make_turned()
        make_base()
        for c in range(chunks):
            if leads and c == chunks - 1:
                fall_copy.wait_recv()
                mate_copy.start()
                if levels > 2:

                    @pl.when(level > 0)
                    def _():
                        fall_copy.start()

                make_factor()
                for d in range(c):
                    store(d, base[d])
            down_copy[c].wait_recv()
            side_copy[c].start()
            base[c] = base[c] - product(turned_own[...], right_operand(own_in[c]))
            side_copy[c].wait_recv()
            value = base[c] - product(turned_next[...], right_operand(beside_in[c]))
            hand_down(c, value)
            if leads and c == chunks - 1:
                store(c, value)
            else:
                base[c] = value
        if not leads:
            mate_copy.wait_recv()
            make_factor()
            for c in range(chunks):
                store(c, base[c])
        for copy in next_copy + up_copy + side_copy:
            copy.wait_send()
        if leads:
            rise_copy.wait_send()
            mate_copy.wait_send()
            if levels > 2:

                @pl.when(level > 0)
                def _():
                    fall_copy.wait_send()
        else:
            pair_copy.wait_send()
        await_down()

    @pl.when(jnp.logical_and(has_up, odd))
    def _():
        climb(True)

    if levels > 2:

        @pl.when(jnp.logical_and(level < levels - 2, even))
        def _():
            climb(False)


def per_device(factor_inv, update_blocks, update_rows, right_side):
    levels = lax.axis_size("level")
    subs = lax.axis_size("sub")
    width = factor_inv.shape[-1]
    columns = right_side.shape[-1]
    slots, block_rows = update_blocks.shape[2:4]
    chunks = columns // LANES
    hubs = subs // 2
    piece = pltpu.VMEM((chunks, width, LANES), jnp.float32)
    wide = pltpu.VMEM((width, 3 * width), jnp.bfloat16)
    line = pltpu.VMEM((1, columns), jnp.float32)
    chunk_sem = pltpu.SemaphoreType.DMA((chunks,))
    in_hbm = pl.BlockSpec(memory_space=pltpu.HBM)
    held = [
        pltpu.with_memory_space_constraint(array, pltpu.HBM)
        for array in (update_rows[0, 0], factor_inv[0, 0], update_blocks[0, 0], right_side[0, 0])
    ]
    value = pl.pallas_call(
        functools.partial(kernel, levels, subs),
        out_shape=jax.ShapeDtypeStruct((width, columns), jnp.float32),
        in_specs=[in_hbm] * 4,
        out_specs=pl.BlockSpec(memory_space=pltpu.VMEM),
        scratch_shapes=[
            pltpu.SMEM((slots,), jnp.int32),
            pltpu.VMEM((width, width), jnp.float32),
            pltpu.VMEM((slots, block_rows, width), jnp.float32),
            piece,
            pltpu.VMEM((chunks, 3 * width, LANES), jnp.bfloat16),
        ]
        + [wide] * 6
        + [piece] * 8
        + [
            pltpu.VMEM((width // 2, width // 2), jnp.float32),
            pltpu.VMEM((width // 2, width), jnp.float32),
            piece,
        ]
        + [line] * 4
        + [pltpu.VMEM((hubs - 1, 1, columns), jnp.float32)]
        + [line] * 2
        + [pltpu.SemaphoreType.DMA((3 + chunks,))]
        + [pltpu.SemaphoreType.DMA((2 + chunks,))] * 2
        + [chunk_sem] * 8
        + [pltpu.SemaphoreType.DMA((4,))] * 2
        + [pltpu.SemaphoreType.DMA((hubs - 1,))] * 2,
        compiler_params=pltpu.CompilerParams(
            collective_id=0, has_side_effects=True, vmem_limit_bytes=32 * 1024 * 1024
        ),
        name="staircase",
    )(*held)
    return value[None, None]


def solution(mesh):
    return jax.shard_map(
        per_device,
        mesh=mesh,
        in_specs=(
            P("level", "sub", None, None),
            P("level", "sub", None, None, None),
            P("level", "sub", None),
            P("level", "sub", None, None),
        ),
        out_specs=P("level", "sub", None, None),
        check_vma=False,
    )
```

```python
import functools

import jax
import jax.numpy as jnp
from jax import lax
from jax.experimental import pallas as pl
from jax.experimental.pallas import tpu as pltpu
from jax.sharding import PartitionSpec as P

LANES = 128
MESH = pl.DeviceIdType.MESH


def halves(value):
    high = value.astype(jnp.bfloat16)
    low = (value - high.astype(jnp.float32)).astype(jnp.bfloat16)
    return high, low


def left_operand(matrix):
    high, low = halves(matrix)
    return jnp.concatenate([high, low, high], axis=1)


def right_operand(values):
    high, low = halves(values)
    return jnp.concatenate([high, high, low], axis=0)


def product(left, right):
    return jnp.dot(left, right, preferred_element_type=jnp.float32)


def kernel(
    levels,
    subs,
    rows_hbm,
    inverse_hbm,
    blocks_hbm,
    rhs_hbm,
    x_ref,
    rows,
    inverse,
    blocks,
    rhs,
    operands,
    spread_own,
    spread_next,
    turned_own,
    turned_next,
    gram,
    gram_top,
    base,
    own,
    next_out,
    next_in,
    up_in,
    own_in,
    beside_in,
    solved,
    top_corner,
    top_rows,
    top_rhs,
    part,
    pair_in,
    rise_in,
    gathered,
    hub_in,
    total_in,
    factor,
    load_sem,
    give_send,
    give_recv,
    next_send,
    next_recv,
    up_send,
    up_recv,
    down_send,
    down_recv,
    side_send,
    side_recv,
    sums_send,
    sums_recv,
    hub_send,
    hub_recv,
):
    level = lax.axis_index("level")
    sub = lax.axis_index("sub")
    chunks = rhs.shape[1] // LANES
    width = inverse.shape[0]
    half = width // 2
    slots = blocks.shape[0]
    hubs = subs // 2
    right = {"sub": lax.rem(sub + 1, subs)}
    left = {"sub": lax.rem(sub + subs - 1, subs)}
    above = {"level": level + 1}
    below = {"level": level - 1}
    others = [{"sub": lax.rem(sub + 2 * j, subs)} for j in range(1, hubs)]
    even = lax.rem(sub, 2) == 0
    odd = jnp.logical_not(even)
    is_top = level == levels - 1
    has_up = level < levels - 1
    is_host = jnp.logical_and(level == levels - 2, even)

    rows_load = pltpu.make_async_copy(rows_hbm, rows, load_sem.at[0])
    block_load = pltpu.make_async_copy(blocks_hbm, blocks, load_sem.at[1])
    inverse_load = pltpu.make_async_copy(inverse_hbm, inverse, load_sem.at[2])
    rhs_load = pltpu.make_async_copy(rhs_hbm, rhs, load_sem.at[3])
    spans = [pl.ds(c * LANES, LANES) for c in range(chunks)]

    barrier = pltpu.get_barrier_semaphore()

    def greet(device):
        pl.semaphore_signal(barrier, inc=1, device_id=device, device_id_type=MESH)

    @pl.when(has_up)
    def _():
        greet(left)
        greet(above)
        rows_load.start()
        block_load.start()

    @pl.when(jnp.logical_and(has_up, even))
    def _():
        greet(right)

    @pl.when(level > 0)
    def _():
        greet(below)

    @pl.when(jnp.logical_and(is_top, even))
    def _():
        greet(right)

    @pl.when(jnp.logical_and(is_top, odd))
    def _():
        greet(left)
        for device in others:
            greet(device)

    greetings = jnp.where(even, 1, jnp.where(is_top, hubs, 2)) + jnp.where(has_up, 1, 0)
    greetings += jnp.where(level > 0, 1, 0)

    inverse_load.start()
    rhs_load.start()

    def remote(source, target, send, recv, device):
        return pltpu.make_async_remote_copy(
            src_ref=source,
            dst_ref=target,
            send_sem=send,
            recv_sem=recv,
            device_id=device,
            device_id_type=MESH,
        )

    def chunk_copies(source, target, send, recv, device):
        return [
            remote(source.at[c], target.at[c], send, recv.at[c], device) for c in range(chunks)
        ]

    def all_sent(array, send):
        remote(array, array, send, send, left).wait_send()

    give_copy = [
        remote(
            inverse_hbm.at[pl.ds(0, half), pl.ds(0, half)],
            top_corner,
            give_send.at[0],
            give_recv.at[0],
            below,
        ),
        remote(
            inverse_hbm.at[pl.ds(half, half)], top_rows, give_send.at[1], give_recv.at[1], below
        ),
    ]
    for c in range(chunks):
        give_copy.append(
            remote(
                rhs_hbm.at[:, pl.ds(c * LANES, LANES)],
                top_rhs.at[c],
                give_send.at[2],
                down_recv.at[c],
                below,
            )
        )
    next_copy = chunk_copies(next_out, next_in, next_send, next_recv, right)
    up_copy = chunk_copies(own, up_in, up_send, up_recv, above)
    lift_copy = chunk_copies(own_in, solved, up_send, up_recv, above)
    down_copy = chunk_copies(solved, own_in, down_send, down_recv, below)
    side_copy = chunk_copies(own_in, beside_in, side_send, side_recv, left)
    pair_copy = remote(part, pair_in, sums_send.at[0], sums_recv.at[0], right)
    rise_copy = remote(gathered, rise_in, sums_send.at[1], sums_recv.at[1], above)
    fall_copy = remote(total_in, total_in, sums_send.at[2], sums_recv.at[2], below)
    mate_copy = remote(total_in, total_in, sums_send.at[3], sums_recv.at[2], left)
    hub_copy = [
        remote(gathered, hub_in.at[j], hub_send, hub_recv, others[j]) for j in range(hubs - 1)
    ]
    hubs_all = remote(hub_in, hub_in, hub_send, hub_recv, left)

    def placed(slot):
        found = jnp.int32(0)
        for k in range(slots):
            found = jnp.where(rows[k] == slot, k, found)
        return blocks[found]

    def spread_matrix(first):
        picked = [placed(first + d) for d in range(slots // 2)]
        ordered = jnp.concatenate(picked, axis=0)
        return product(left_operand(ordered), right_operand(inverse[...]))

    def squared(matrix):
        return left_operand(product(left_operand(matrix.T), right_operand(matrix)))

    def make_part():
        for span in spans:
            value = rhs[:, span]
            part[:, span] = jnp.sum(value * value, axis=0, keepdims=True)

    def gather_pair():
        pair_copy.wait_recv()
        if levels > 2:

            @pl.when(level > 0)
            def _():
                rise_copy.wait_recv()

            gathered[...] = part[...] + pair_in[...] + jnp.where(level > 0, rise_in[...], 0.0)
        else:
            gathered[...] = part[...] + pair_in[...]

    def make_factor():
        factor[...] = 1.0 / jnp.sqrt(total_in[...] / (levels * subs * width) + 1e-06)

    def store(c, value):
        x_ref[:, spans[c]] = value * factor[:, spans[c]]

    @pl.when(jnp.logical_and(is_top, even))
    def _():
        pl.semaphore_wait(barrier, greetings)
        for copy in give_copy:
            copy.start()
        rhs_load.wait()
        make_part()
        pair_copy.start()
        inverse_load.wait()
        pair_copy.wait_send()
        give_copy[0].wait_send()
        give_copy[1].wait_send()
        all_sent(top_rhs, give_send.at[2])
        mate_copy.wait_recv()
        make_factor()
        for c in range(chunks):
            lift_copy[c].wait_recv()
            store(c, solved[c])

    @pl.when(jnp.logical_and(is_top, odd))
    def _():
        rhs_load.wait()
        make_part()
        inverse_load.wait()
        gram[...] = squared(inverse[...])
        pl.semaphore_wait(barrier, greetings)

        def solve(c):
            up_copy[c].wait_recv()
            solved[c] = product(gram[...], right_operand(rhs[:, spans[c]] - up_in[c]))
            down_copy[c].start()

        pair_copy.wait_recv()
        rise_copy.wait_recv()
        gathered[...] = part[...] + pair_in[...] + rise_in[...]
        for copy in hub_copy:
            copy.start()
        for c in range(chunks - 1):
            solve(c)
        hubs_all.wait_recv()
        value = gathered[...]
        for j in range(hubs - 1):
            value = value + hub_in[j]
        total_in[...] = value
        fall_copy.start()
        mate_copy.start()
        solve(chunks - 1)
        make_factor()
        for c in range(chunks):
            store(c, solved[c])
        hubs_all.wait_send()
        fall_copy.wait_send()
        mate_copy.wait_send()
        all_sent(solved, down_send)

    def make_next():
        matrix = spread_matrix(slots // 2)
        spread_next[...] = left_operand(matrix)

    def make_own():
        matrix = spread_matrix(0)
        spread_own[...] = left_operand(matrix)

    def make_turned():
        for matrix, turned in ((spread_own, turned_own), (spread_next, turned_next)):
            for piece in range(3):
                span = pl.ds(piece * width, width)
                turned[:, span] = matrix[:, span].T

    def take(c):
        value = rhs[:, spans[c]]
        if levels > 2:

            @pl.when(level > 0)
            def _():
                up_copy[c].wait_recv()

            value = value - jnp.where(level > 0, up_in[c], 0.0)
        operands[c] = right_operand(value)

    def make_base():
        gram[...] = squared(inverse[...])
        for c in range(chunks):
            base[c] = product(gram[...], operands[c])

    def send_next(c):
        take(c)
        next_out[c] = product(spread_next[...], operands[c])
        if c == 0:
            make_part()
            pl.semaphore_wait(barrier, greetings)

            @pl.when(even)
            def _():
                pair_copy.start()

        next_copy[c].start()

    def start_up():
        rows_load.wait()
        block_load.wait()
        inverse_load.wait()
        make_next()
        rhs_load.wait()

    def hand_down(c, value):
        if levels > 2:

            @pl.when(level > 0)
            def _():
                solved[c] = value
                down_copy[c].start()

    def await_down():
        if levels > 2:

            @pl.when(level > 0)
            def _():
                all_sent(solved, down_send)

    @pl.when(is_host)
    def _():
        start_up()
        for c in range(chunks):
            send_next(c)
        make_own()
        for c in range(chunks):
            own[c] = product(spread_own[...], operands[c])
        make_turned()
        make_base()
        give_copy[0].wait_recv()
        give_copy[1].wait_recv()
        corner = jnp.concatenate([top_corner[...], jnp.zeros((half, half), jnp.float32)], axis=1)
        gram_top[...] = squared(jnp.concatenate([corner, top_rows[...]], axis=0))
        for c in range(chunks):
            next_copy[c].wait_recv()
            give_copy[2 + c].wait_recv()
            operand = right_operand(top_rhs[c] - (own[c] + next_in[c]))
            value = product(gram_top[...], operand)
            own_in[c] = value
            lift_copy[c].start()
            side_copy[c].start()
            base[c] = base[c] - product(turned_own[...], right_operand(value))
        for c in range(chunks):
            if c == chunks - 1:
                mate_copy.wait_recv()
                make_factor()
                for d in range(c):
                    store(d, base[d])
            side_copy[c].wait_recv()
            value = base[c] - product(turned_next[...], right_operand(beside_in[c]))
            hand_down(c, value)
            if c == chunks - 1:
                store(c, value)
            else:
                base[c] = value
        pair_copy.wait_send()
        all_sent(next_out, next_send)
        all_sent(own_in, up_send)
        all_sent(own_in, side_send)
        await_down()

    def climb(leads):
        start_up()
        early = min(2, chunks)
        for c in range(early):
            send_next(c)
        make_own()
        for c in range(early):
            own[c] = product(spread_own[...], operands[c])
        if leads:
            gather_pair()
            rise_copy.start()
        for c in range(early):
            next_copy[c].wait_recv()
            own[c] = own[c] + next_in[c]
            up_copy[c].start()
        for c in range(early, chunks):
            send_next(c)
            own[c] = product(spread_own[...], operands[c])
        for c in range(early, chunks):
            next_copy[c].wait_recv()
            own[c] = own[c] + next_in[c]
            up_copy[c].start()
        make_turned()
        make_base()
        for c in range(chunks):
            if leads and c == chunks - 1:
                fall_copy.wait_recv()
                mate_copy.start()
                if levels > 2:

                    @pl.when(level > 0)
                    def _():
                        fall_copy.start()

                make_factor()
                for d in range(c):
                    store(d, base[d])
            down_copy[c].wait_recv()
            side_copy[c].start()
            base[c] = base[c] - product(turned_own[...], right_operand(own_in[c]))
            side_copy[c].wait_recv()
            value = base[c] - product(turned_next[...], right_operand(beside_in[c]))
            hand_down(c, value)
            if leads and c == chunks - 1:
                store(c, value)
            else:
                base[c] = value
        if not leads:
            mate_copy.wait_recv()
            make_factor()
            for c in range(chunks):
                store(c, base[c])
        all_sent(next_out, next_send)
        all_sent(own, up_send)
        all_sent(own_in, side_send)
        if leads:
            rise_copy.wait_send()
            mate_copy.wait_send()
            if levels > 2:

                @pl.when(level > 0)
                def _():
                    fall_copy.wait_send()
        else:
            pair_copy.wait_send()
        await_down()

    @pl.when(jnp.logical_and(has_up, odd))
    def _():
        climb(True)

    if levels > 2:

        @pl.when(jnp.logical_and(level < levels - 2, even))
        def _():
            climb(False)


def per_device(factor_inv, update_blocks, update_rows, right_side):
    levels = lax.axis_size("level")
    subs = lax.axis_size("sub")
    width = factor_inv.shape[-1]
    columns = right_side.shape[-1]
    slots, block_rows = update_blocks.shape[2:4]
    chunks = columns // LANES
    hubs = subs // 2
    piece = pltpu.VMEM((chunks, width, LANES), jnp.float32)
    wide = pltpu.VMEM((width, 3 * width), jnp.bfloat16)
    line = pltpu.VMEM((1, columns), jnp.float32)
    chunk_sem = pltpu.SemaphoreType.DMA((chunks,))
    in_hbm = pl.BlockSpec(memory_space=pltpu.HBM)
    held = [
        pltpu.with_memory_space_constraint(array, pltpu.HBM)
        for array in (update_rows[0, 0], factor_inv[0, 0], update_blocks[0, 0], right_side[0, 0])
    ]
    value = pl.pallas_call(
        functools.partial(kernel, levels, subs),
        out_shape=jax.ShapeDtypeStruct((width, columns), jnp.float32),
        in_specs=[in_hbm] * 4,
        out_specs=pl.BlockSpec(memory_space=pltpu.VMEM),
        scratch_shapes=[
            pltpu.SMEM((slots,), jnp.int32),
            pltpu.VMEM((width, width), jnp.float32),
            pltpu.VMEM((slots, block_rows, width), jnp.float32),
            pltpu.VMEM((width, columns), jnp.float32),
            pltpu.VMEM((chunks, 3 * width, LANES), jnp.bfloat16),
        ]
        + [wide] * 6
        + [piece] * 8
        + [
            pltpu.VMEM((width // 2, width // 2), jnp.float32),
            pltpu.VMEM((width // 2, width), jnp.float32),
            piece,
        ]
        + [line] * 4
        + [pltpu.VMEM((hubs - 1, 1, columns), jnp.float32)]
        + [line] * 2
        + [pltpu.SemaphoreType.DMA((4,)), pltpu.SemaphoreType.DMA((3,))]
        + [pltpu.SemaphoreType.DMA((2,))]
        + [pltpu.SemaphoreType.DMA, chunk_sem] * 4
        + [pltpu.SemaphoreType.DMA((4,)), pltpu.SemaphoreType.DMA((3,))]
        + [pltpu.SemaphoreType.DMA] * 2,
        compiler_params=pltpu.CompilerParams(
            collective_id=0, has_side_effects=True, vmem_limit_bytes=32 * 1024 * 1024
        ),
        name="staircase",
    )(*held)
    return value[None, None]


def solution(mesh):
    return jax.shard_map(
        per_device,
        mesh=mesh,
        in_specs=(
            P("level", "sub", None, None),
            P("level", "sub", None, None, None),
            P("level", "sub", None),
            P("level", "sub", None, None),
        ),
        out_specs=P("level", "sub", None, None),
        check_vma=False,
    )
```

```python
import functools

import jax
import jax.numpy as jnp
from jax import lax
from jax.experimental import pallas as pl
from jax.experimental.pallas import tpu as pltpu
from jax.sharding import PartitionSpec as P

LANES = 128
MESH = pl.DeviceIdType.MESH


def halves(value):
    high = value.astype(jnp.bfloat16)
    low = (value - high.astype(jnp.float32)).astype(jnp.bfloat16)
    return high, low


def left_operand(matrix):
    high, low = halves(matrix)
    return jnp.concatenate([high, low, high], axis=1)


def right_operand(values):
    high, low = halves(values)
    return jnp.concatenate([high, high, low], axis=0)


def product(left, right):
    return jnp.dot(left, right, preferred_element_type=jnp.float32)


def kernel(
    levels,
    subs,
    rows_hbm,
    inverse_hbm,
    blocks_hbm,
    rhs_hbm,
    x_ref,
    rows,
    inverse,
    blocks,
    rhs,
    operands,
    spread_own,
    spread_next,
    turned_own,
    turned_next,
    gram,
    gram_top,
    base,
    own,
    next_out,
    next_in,
    up_in,
    own_in,
    beside_in,
    solved,
    packed,
    top_corner,
    top_rhs,
    part,
    pair_in,
    rise_in,
    gathered,
    hub_in,
    total_in,
    factor,
    load_sem,
    give_send,
    give_recv,
    next_send,
    next_recv,
    up_send,
    up_recv,
    down_send,
    down_recv,
    side_send,
    side_recv,
    sums_send,
    sums_recv,
    hub_send,
    hub_recv,
    clear_sem,
):
    level = lax.axis_index("level")
    sub = lax.axis_index("sub")
    chunks = rhs.shape[1] // LANES
    width = inverse.shape[0]
    half = width // 2
    slots = blocks.shape[0]
    hubs = subs // 2
    right = {"sub": lax.rem(sub + 1, subs)}
    left = {"sub": lax.rem(sub + subs - 1, subs)}
    above = {"level": level + 1}
    below = {"level": level - 1}
    others = [{"sub": lax.rem(sub + 2 * j, subs)} for j in range(1, hubs)]
    even = lax.rem(sub, 2) == 0
    odd = jnp.logical_not(even)
    is_top = level == levels - 1
    has_up = level < levels - 1
    is_host = jnp.logical_and(level == levels - 2, even)

    rows_load = pltpu.make_async_copy(rows_hbm, rows, load_sem.at[0])
    block_load = pltpu.make_async_copy(blocks_hbm, blocks, load_sem.at[1])
    inverse_load = pltpu.make_async_copy(inverse_hbm, inverse, load_sem.at[2])
    rhs_load = pltpu.make_async_copy(rhs_hbm, rhs, load_sem.at[3])
    spans = [pl.ds(c * LANES, LANES) for c in range(chunks)]

    barrier = pltpu.get_barrier_semaphore()

    def greet(device):
        pl.semaphore_signal(barrier, inc=1, device_id=device, device_id_type=MESH)

    @pl.when(has_up)
    def _():
        greet(left)
        greet(above)
        rows_load.start()
        block_load.start()

    @pl.when(jnp.logical_and(has_up, even))
    def _():
        greet(right)

    @pl.when(level > 0)
    def _():
        greet(below)

    @pl.when(jnp.logical_and(is_top, even))
    def _():
        greet(right)

    @pl.when(jnp.logical_and(is_top, odd))
    def _():
        greet(left)
        for device in others:
            greet(device)

    greetings = jnp.where(even, 1, jnp.where(is_top, hubs, 2)) + jnp.where(has_up, 1, 0)
    greetings += jnp.where(level > 0, 1, 0)

    inverse_load.start()

    @pl.when(jnp.logical_not(jnp.logical_and(is_top, even)))
    def _():
        rhs_load.start()

    def remote(source, target, send, recv, device):
        return pltpu.make_async_remote_copy(
            src_ref=source,
            dst_ref=target,
            send_sem=send,
            recv_sem=recv,
            device_id=device,
            device_id_type=MESH,
        )

    def chunk_copies(source, target, send, recv, device):
        return [
            remote(source.at[c], target.at[c], send, recv.at[c], device) for c in range(chunks)
        ]

    def all_sent(array, send):
        remote(array, array, send, send, left).wait_send()

    corner_copy = remote(
        inverse_hbm.at[pl.ds(half, half), pl.ds(0, half)],
        top_corner,
        give_send.at[0],
        give_recv.at[0],
        below,
    )
    packed_copy = remote(packed, packed, give_send.at[1], give_recv.at[1], below)
    give_copy = [
        remote(
            rhs_hbm.at[:, spans[c]],
            top_rhs.at[c],
            give_send.at[2 if c < chunks - 1 else 3],
            down_recv.at[c],
            below,
        )
        for c in range(chunks)
    ]
    next_copy = chunk_copies(next_out, next_in, next_send, next_recv, right)
    up_copy = chunk_copies(own, up_in, up_send, up_recv, above)
    lift_copy = chunk_copies(own_in, solved, up_send, up_recv, above)
    down_copy = chunk_copies(solved, own_in, down_send, down_recv, below)
    side_copy = chunk_copies(own_in, beside_in, side_send, side_recv, left)
    pair_copy = remote(part, pair_in, sums_send.at[0], sums_recv.at[0], right)
    rise_copy = remote(gathered, rise_in, sums_send.at[1], sums_recv.at[1], above)
    fall_copy = remote(total_in, total_in, sums_send.at[2], sums_recv.at[2], below)
    mate_copy = remote(total_in, total_in, sums_send.at[3], sums_recv.at[2], left)
    hub_copy = [
        remote(gathered, hub_in.at[j], hub_send, hub_recv, others[j]) for j in range(hubs - 1)
    ]
    hubs_all = remote(hub_in, hub_in, hub_send, hub_recv, left)

    def placed(slot):
        found = jnp.int32(0)
        for k in range(slots):
            found = jnp.where(rows[k] == slot, k, found)
        return blocks[found]

    def spread_matrix(first):
        picked = [placed(first + d) for d in range(slots // 2)]
        ordered = jnp.concatenate(picked, axis=0)
        return product(left_operand(ordered), right_operand(inverse[...]))

    def squared(matrix):
        return left_operand(product(left_operand(matrix.T), right_operand(matrix)))

    def make_part():
        for span in spans:
            value = rhs[:, span]
            part[:, span] = jnp.sum(value * value, axis=0, keepdims=True)

    def gather_pair():
        pair_copy.wait_recv()
        if levels > 2:

            @pl.when(level > 0)
            def _():
                rise_copy.wait_recv()

            gathered[...] = part[...] + pair_in[...] + jnp.where(level > 0, rise_in[...], 0.0)
        else:
            gathered[...] = part[...] + pair_in[...]

    def make_factor():
        factor[...] = 1.0 / jnp.sqrt(total_in[...] / (levels * subs * width) + 1e-06)

    def store(c, value):
        x_ref[:, spans[c]] = value * factor[:, spans[c]]

    block_row = lax.broadcasted_iota(jnp.int32, (half, half), 0)
    block_column = lax.broadcasted_iota(jnp.int32, (half, half), 1)

    def pack():
        first = inverse[pl.ds(0, half), pl.ds(0, half)]
        second = inverse[pl.ds(half, half), pl.ds(half, half)]
        packed[pl.ds(0, half)] = jnp.where(block_row >= block_column, first, second.T)
        diagonal = jnp.where(block_row == block_column, second, 0.0)
        packed[pl.ds(half, 8)] = jnp.broadcast_to(
            jnp.sum(diagonal, axis=0, keepdims=True), (8, half)
        )

    def unpack():
        both = packed[pl.ds(0, half)]
        diagonal = packed[pl.ds(half, 1)]
        zero = jnp.zeros((half, half), jnp.float32)
        first = jnp.where(block_row >= block_column, both, 0.0)
        second = jnp.where(block_row < block_column, both, 0.0)
        second = jnp.where(block_row == block_column, diagonal, second).T
        upper = jnp.concatenate([first, zero], axis=1)
        lower = jnp.concatenate([top_corner[...], second], axis=1)
        return jnp.concatenate([upper, lower], axis=0)

    @pl.when(jnp.logical_and(is_top, even))
    def _():
        pl.semaphore_wait(barrier, greetings)
        give_copy[0].start()
        corner_copy.start()
        rhs_load.start()
        inverse_load.wait()
        pack()
        packed_copy.start()
        for copy in give_copy[1:]:
            copy.start()
        rhs_load.wait()
        make_part()
        pair_copy.start()
        pair_copy.wait_send()
        corner_copy.wait_send()
        packed_copy.wait_send()
        all_sent(top_rhs.at[pl.ds(0, chunks - 1)], give_send.at[2])
        pl.semaphore_signal(clear_sem, inc=1, device_id=right, device_id_type=MESH)
        give_copy[chunks - 1].wait_send()
        mate_copy.wait_recv()
        make_factor()
        for c in range(chunks):
            lift_copy[c].wait_recv()
            store(c, solved[c])

    @pl.when(jnp.logical_and(is_top, odd))
    def _():
        rhs_load.wait()
        make_part()
        inverse_load.wait()
        gram[...] = squared(inverse[...])
        pl.semaphore_wait(barrier, greetings)

        def solve(c):
            up_copy[c].wait_recv()
            solved[c] = product(gram[...], right_operand(rhs[:, spans[c]] - up_in[c]))
            if c == 0:
                pl.semaphore_wait(clear_sem, 1)
            down_copy[c].start()

        pair_copy.wait_recv()
        rise_copy.wait_recv()
        gathered[...] = part[...] + pair_in[...] + rise_in[...]
        for copy in hub_copy:
            copy.start()
        for c in range(chunks - 1):
            solve(c)
        hubs_all.wait_recv()
        value = gathered[...]
        for j in range(hubs - 1):
            value = value + hub_in[j]
        total_in[...] = value
        fall_copy.start()
        mate_copy.start()
        solve(chunks - 1)
        make_factor()
        for c in range(chunks):
            store(c, solved[c])
        hubs_all.wait_send()
        fall_copy.wait_send()
        mate_copy.wait_send()
        all_sent(solved, down_send)

    def make_next():
        matrix = spread_matrix(slots // 2)
        spread_next[...] = left_operand(matrix)

    def make_own():
        matrix = spread_matrix(0)
        spread_own[...] = left_operand(matrix)

    def make_turned():
        for matrix, turned in ((spread_own, turned_own), (spread_next, turned_next)):
            for piece in range(3):
                span = pl.ds(piece * width, width)
                turned[:, span] = matrix[:, span].T

    def take(c):
        value = rhs[:, spans[c]]
        if levels > 2:

            @pl.when(level > 0)
            def _():
                up_copy[c].wait_recv()

            value = value - jnp.where(level > 0, up_in[c], 0.0)
        operands[c] = right_operand(value)

    def make_base():
        gram[...] = squared(inverse[...])
        for c in range(chunks):
            base[c] = product(gram[...], operands[c])

    def send_next(c):
        take(c)
        next_out[c] = product(spread_next[...], operands[c])
        if c == 0:
            make_part()
            pl.semaphore_wait(barrier, greetings)

            @pl.when(even)
            def _():
                pair_copy.start()

        next_copy[c].start()

    def start_up():
        rows_load.wait()
        block_load.wait()
        inverse_load.wait()
        make_next()
        rhs_load.wait()

    def hand_down(c, value):
        if levels > 2:

            @pl.when(level > 0)
            def _():
                solved[c] = value
                down_copy[c].start()

    def await_down():
        if levels > 2:

            @pl.when(level > 0)
            def _():
                all_sent(solved, down_send)

    @pl.when(is_host)
    def _():
        start_up()
        for c in range(chunks):
            send_next(c)
        make_own()
        for c in range(chunks):
            own[c] = product(spread_own[...], operands[c])
        make_turned()
        make_base()
        corner_copy.wait_recv()
        packed_copy.wait_recv()
        gram_top[...] = squared(unpack())
        for c in range(chunks):
            next_copy[c].wait_recv()
            give_copy[c].wait_recv()
            operand = right_operand(top_rhs[c] - (own[c] + next_in[c]))
            value = product(gram_top[...], operand)
            own_in[c] = value
            side_copy[c].start()
            lift_copy[c].start()
            base[c] = base[c] - product(turned_own[...], right_operand(value))
        for c in range(chunks):
            if c == chunks - 1:
                mate_copy.wait_recv()
                make_factor()
                for d in range(c):
                    store(d, base[d])
            side_copy[c].wait_recv()
            value = base[c] - product(turned_next[...], right_operand(beside_in[c]))
            hand_down(c, value)
            if c == chunks - 1:
                store(c, value)
            else:
                base[c] = value
        pair_copy.wait_send()
        all_sent(next_out, next_send)
        all_sent(own_in, up_send)
        all_sent(own_in, side_send)
        await_down()

    def climb(leads):
        start_up()
        early = min(2, chunks)
        for c in range(early):
            send_next(c)
        make_own()
        for c in range(early):
            own[c] = product(spread_own[...], operands[c])
        if leads:
            gather_pair()
            rise_copy.start()
        for c in range(early):
            next_copy[c].wait_recv()
            own[c] = own[c] + next_in[c]
            up_copy[c].start()
        for c in range(early, chunks):
            send_next(c)
            own[c] = product(spread_own[...], operands[c])
        for c in range(early, chunks):
            next_copy[c].wait_recv()
            own[c] = own[c] + next_in[c]
            up_copy[c].start()
        make_turned()
        make_base()

        def spread_total():
            if leads:
                fall_copy.wait_recv()
                mate_copy.start()
                if levels > 2:

                    @pl.when(level > 0)
                    def _():
                        fall_copy.start()

                make_factor()

        def own_part(c):
            down_copy[c].wait_recv()
            side_copy[c].start()
            base[c] = base[c] - product(turned_own[...], right_operand(own_in[c]))

        def beside_part(c):
            side_copy[c].wait_recv()
            value = base[c] - product(turned_next[...], right_operand(beside_in[c]))
            hand_down(c, value)
            if leads and c >= chunks - 2:
                store(c, value)
            else:
                base[c] = value

        early = max(chunks - 2, 0)
        for c in range(chunks - 1):
            own_part(c)
            if c > 0:
                beside_part(c - 1)
        spread_total()
        if leads:
            for c in range(early):
                store(c, base[c])
        own_part(chunks - 1)
        for c in range(early, chunks):
            beside_part(c)
        if not leads:
            mate_copy.wait_recv()
            make_factor()
            for c in range(chunks):
                store(c, base[c])
        all_sent(next_out, next_send)
        all_sent(own, up_send)
        all_sent(own_in, side_send)
        if leads:
            rise_copy.wait_send()
            mate_copy.wait_send()
            if levels > 2:

                @pl.when(level > 0)
                def _():
                    fall_copy.wait_send()
        else:
            pair_copy.wait_send()
        await_down()

    @pl.when(jnp.logical_and(has_up, odd))
    def _():
        climb(True)

    if levels > 2:

        @pl.when(jnp.logical_and(level < levels - 2, even))
        def _():
            climb(False)


def per_device(factor_inv, update_blocks, update_rows, right_side):
    levels = lax.axis_size("level")
    subs = lax.axis_size("sub")
    width = factor_inv.shape[-1]
    columns = right_side.shape[-1]
    slots, block_rows = update_blocks.shape[2:4]
    chunks = columns // LANES
    hubs = subs // 2
    piece = pltpu.VMEM((chunks, width, LANES), jnp.float32)
    wide = pltpu.VMEM((width, 3 * width), jnp.bfloat16)
    line = pltpu.VMEM((1, columns), jnp.float32)
    chunk_sem = pltpu.SemaphoreType.DMA((chunks,))
    in_hbm = pl.BlockSpec(memory_space=pltpu.HBM)
    held = [
        pltpu.with_memory_space_constraint(array, pltpu.HBM)
        for array in (update_rows[0, 0], factor_inv[0, 0], update_blocks[0, 0], right_side[0, 0])
    ]
    value = pl.pallas_call(
        functools.partial(kernel, levels, subs),
        out_shape=jax.ShapeDtypeStruct((width, columns), jnp.float32),
        in_specs=[in_hbm] * 4,
        out_specs=pl.BlockSpec(memory_space=pltpu.VMEM),
        scratch_shapes=[
            pltpu.SMEM((slots,), jnp.int32),
            pltpu.VMEM((width, width), jnp.float32),
            pltpu.VMEM((slots, block_rows, width), jnp.float32),
            pltpu.VMEM((width, columns), jnp.float32),
            pltpu.VMEM((chunks, 3 * width, LANES), jnp.bfloat16),
        ]
        + [wide] * 6
        + [piece] * 8
        + [
            pltpu.VMEM((width // 2 + 8, width // 2), jnp.float32),
            pltpu.VMEM((width // 2, width // 2), jnp.float32),
            piece,
        ]
        + [line] * 4
        + [pltpu.VMEM((hubs - 1, 1, columns), jnp.float32)]
        + [line] * 2
        + [pltpu.SemaphoreType.DMA((4,)), pltpu.SemaphoreType.DMA((4,))]
        + [pltpu.SemaphoreType.DMA((2,))]
        + [pltpu.SemaphoreType.DMA, chunk_sem] * 4
        + [pltpu.SemaphoreType.DMA((4,)), pltpu.SemaphoreType.DMA((3,))]
        + [pltpu.SemaphoreType.DMA] * 2
        + [pltpu.SemaphoreType.REGULAR],
        compiler_params=pltpu.CompilerParams(
            collective_id=0, has_side_effects=True, vmem_limit_bytes=32 * 1024 * 1024
        ),
        name="staircase",
    )(*held)
    return value[None, None]


def solution(mesh):
    return jax.shard_map(
        per_device,
        mesh=mesh,
        in_specs=(
            P("level", "sub", None, None),
            P("level", "sub", None, None, None),
            P("level", "sub", None),
            P("level", "sub", None, None),
        ),
        out_specs=P("level", "sub", None, None),
        check_vma=False,
    )
```

```python
import functools

import jax
import jax.numpy as jnp
from jax import lax
from jax.experimental import pallas as pl
from jax.experimental.pallas import tpu as pltpu
from jax.sharding import PartitionSpec as P

LANES = 128
DETOUR = {"sender": 2, "relay": 5, "receiver": 1, "chunks": 1}
MESH = pl.DeviceIdType.MESH


def halves(value):
    high = value.astype(jnp.bfloat16)
    low = (value - high.astype(jnp.float32)).astype(jnp.bfloat16)
    return high, low


def left_operand(matrix):
    high, low = halves(matrix)
    return jnp.concatenate([high, low, high], axis=1)


def right_operand(values):
    high, low = halves(values)
    return jnp.concatenate([high, high, low], axis=0)


def product(left, right):
    return jnp.dot(left, right, preferred_element_type=jnp.float32)


def kernel(
    levels,
    subs,
    rows_hbm,
    inverse_hbm,
    blocks_hbm,
    rhs_hbm,
    x_ref,
    rows,
    inverse,
    blocks,
    rhs,
    operands,
    spread_own,
    spread_next,
    turned_own,
    turned_next,
    gram,
    gram_top,
    base,
    own,
    next_out,
    next_in,
    up_in,
    own_in,
    beside_in,
    relayed,
    solved,
    packed,
    top_corner,
    top_rhs,
    part,
    pair_in,
    rise_in,
    gathered,
    hub_in,
    total_in,
    factor,
    load_sem,
    give_send,
    give_recv,
    next_send,
    next_recv,
    up_send,
    up_recv,
    down_send,
    down_recv,
    side_send,
    side_recv,
    sums_send,
    sums_recv,
    hub_send,
    hub_recv,
    clear_sem,
    relay_send,
    relay_recv,
):
    level = lax.axis_index("level")
    sub = lax.axis_index("sub")
    chunks = rhs.shape[1] // LANES
    width = inverse.shape[0]
    half = width // 2
    slots = blocks.shape[0]
    hubs = subs // 2
    right = {"sub": lax.rem(sub + 1, subs)}
    left = {"sub": lax.rem(sub + subs - 1, subs)}
    detours = relayed.shape[0] if subs > DETOUR["relay"] else 0
    detour = {name: {"sub": DETOUR[name]} for name in ("sender", "relay", "receiver")}
    above = {"level": level + 1}
    below = {"level": level - 1}
    others = [{"sub": lax.rem(sub + 2 * j, subs)} for j in range(1, hubs)]
    even = lax.rem(sub, 2) == 0
    odd = jnp.logical_not(even)
    is_top = level == levels - 1
    has_up = level < levels - 1
    is_host = jnp.logical_and(level == levels - 2, even)

    rows_load = pltpu.make_async_copy(rows_hbm, rows, load_sem.at[0])
    block_load = pltpu.make_async_copy(blocks_hbm, blocks, load_sem.at[1])
    inverse_load = pltpu.make_async_copy(inverse_hbm, inverse, load_sem.at[2])
    rhs_load = pltpu.make_async_copy(rhs_hbm, rhs, load_sem.at[3])
    spans = [pl.ds(c * LANES, LANES) for c in range(chunks)]

    barrier = pltpu.get_barrier_semaphore()

    def greet(device):
        pl.semaphore_signal(barrier, inc=1, device_id=device, device_id_type=MESH)

    @pl.when(has_up)
    def _():
        greet(left)
        greet(above)
        rows_load.start()
        block_load.start()

    @pl.when(jnp.logical_and(has_up, even))
    def _():
        greet(right)

    is_sender = jnp.logical_and(has_up, sub == DETOUR["sender"])
    is_relay = jnp.logical_and(has_up, sub == DETOUR["relay"])
    if detours:

        @pl.when(is_relay)
        def _():
            greet(detour["sender"])

        @pl.when(jnp.logical_and(has_up, sub == DETOUR["receiver"]))
        def _():
            greet(detour["relay"])

    @pl.when(level > 0)
    def _():
        greet(below)

    @pl.when(jnp.logical_and(is_top, even))
    def _():
        greet(right)

    @pl.when(jnp.logical_and(is_top, odd))
    def _():
        greet(left)
        for device in others:
            greet(device)

    greetings = jnp.where(even, 1, jnp.where(is_top, hubs, 2)) + jnp.where(has_up, 1, 0)
    greetings += jnp.where(level > 0, 1, 0)
    if detours:
        greetings += jnp.where(jnp.logical_or(is_sender, is_relay), 1, 0)

    inverse_load.start()

    @pl.when(jnp.logical_not(jnp.logical_and(is_top, even)))
    def _():
        rhs_load.start()

    def remote(source, target, send, recv, device):
        return pltpu.make_async_remote_copy(
            src_ref=source,
            dst_ref=target,
            send_sem=send,
            recv_sem=recv,
            device_id=device,
            device_id_type=MESH,
        )

    def chunk_copies(source, target, send, recv, device):
        return [
            remote(source.at[c], target.at[c], send, recv.at[c], device) for c in range(chunks)
        ]

    def all_sent(array, send):
        remote(array, array, send, send, left).wait_send()

    corner_copy = remote(
        inverse_hbm.at[pl.ds(half, half), pl.ds(0, half)],
        top_corner,
        give_send.at[0],
        give_recv.at[0],
        below,
    )
    packed_copy = remote(packed, packed, give_send.at[1], give_recv.at[1], below)
    give_copy = [
        remote(
            rhs_hbm.at[:, spans[c]],
            top_rhs.at[c],
            give_send.at[2 if c < chunks - 1 else 3],
            down_recv.at[c],
            below,
        )
        for c in range(chunks)
    ]
    next_copy = chunk_copies(next_out, next_in, next_send, next_recv, right)
    up_copy = chunk_copies(own, up_in, up_send, up_recv, above)
    lift_copy = chunk_copies(own_in, solved, up_send, up_recv, above)
    down_copy = chunk_copies(solved, own_in, down_send, down_recv, below)
    side_copy = chunk_copies(own_in, beside_in, side_send, side_recv, left)
    away_copy = [
        remote(own_in.at[c], relayed.at[c], side_send, relay_recv.at[c], detour["relay"])
        for c in range(detours)
    ]
    relay_copy = [
        remote(relayed.at[c], beside_in.at[c], relay_send, side_recv.at[c], detour["receiver"])
        for c in range(detours)
    ]
    pair_copy = remote(part, pair_in, sums_send.at[0], sums_recv.at[0], right)
    rise_copy = remote(gathered, rise_in, sums_send.at[1], sums_recv.at[1], above)
    fall_copy = remote(total_in, total_in, sums_send.at[2], sums_recv.at[2], below)
    mate_copy = remote(total_in, total_in, sums_send.at[3], sums_recv.at[2], left)
    hub_copy = [
        remote(gathered, hub_in.at[j], hub_send, hub_recv, others[j]) for j in range(hubs - 1)
    ]
    hubs_all = remote(hub_in, hub_in, hub_send, hub_recv, left)

    def placed(slot):
        found = jnp.int32(0)
        for k in range(slots):
            found = jnp.where(rows[k] == slot, k, found)
        return blocks[found]

    def spread_matrix(first):
        picked = [placed(first + d) for d in range(slots // 2)]
        ordered = jnp.concatenate(picked, axis=0)
        return product(left_operand(ordered), right_operand(inverse[...]))

    def squared(matrix):
        return left_operand(product(left_operand(matrix.T), right_operand(matrix)))

    def make_part():
        for span in spans:
            value = rhs[:, span]
            part[:, span] = jnp.sum(value * value, axis=0, keepdims=True)

    def gather_pair():
        pair_copy.wait_recv()
        if levels > 2:

            @pl.when(level > 0)
            def _():
                rise_copy.wait_recv()

            gathered[...] = part[...] + pair_in[...] + jnp.where(level > 0, rise_in[...], 0.0)
        else:
            gathered[...] = part[...] + pair_in[...]

    def make_factor():
        factor[...] = 1.0 / jnp.sqrt(total_in[...] / (levels * subs * width) + 1e-06)

    def store(c, value):
        x_ref[:, spans[c]] = value * factor[:, spans[c]]

    block_row = lax.broadcasted_iota(jnp.int32, (half, half), 0)
    block_column = lax.broadcasted_iota(jnp.int32, (half, half), 1)

    def pack():
        first = inverse[pl.ds(0, half), pl.ds(0, half)]
        second = inverse[pl.ds(half, half), pl.ds(half, half)]
        packed[pl.ds(0, half)] = jnp.where(block_row >= block_column, first, second.T)
        diagonal = jnp.where(block_row == block_column, second, 0.0)
        packed[pl.ds(half, 8)] = jnp.broadcast_to(
            jnp.sum(diagonal, axis=0, keepdims=True), (8, half)
        )

    def unpack():
        both = packed[pl.ds(0, half)]
        diagonal = packed[pl.ds(half, 1)]
        zero = jnp.zeros((half, half), jnp.float32)
        first = jnp.where(block_row >= block_column, both, 0.0)
        second = jnp.where(block_row < block_column, both, 0.0)
        second = jnp.where(block_row == block_column, diagonal, second).T
        upper = jnp.concatenate([first, zero], axis=1)
        lower = jnp.concatenate([top_corner[...], second], axis=1)
        return jnp.concatenate([upper, lower], axis=0)

    @pl.when(jnp.logical_and(is_top, even))
    def _():
        pl.semaphore_wait(barrier, greetings)
        give_copy[0].start()
        corner_copy.start()
        rhs_load.start()
        inverse_load.wait()
        pack()
        packed_copy.start()
        for copy in give_copy[1:]:
            copy.start()
        rhs_load.wait()
        make_part()
        pair_copy.start()
        pair_copy.wait_send()
        corner_copy.wait_send()
        packed_copy.wait_send()
        all_sent(top_rhs.at[pl.ds(0, chunks - 1)], give_send.at[2])
        pl.semaphore_signal(clear_sem, inc=1, device_id=right, device_id_type=MESH)
        give_copy[chunks - 1].wait_send()
        mate_copy.wait_recv()
        make_factor()
        for c in range(chunks):
            lift_copy[c].wait_recv()
            store(c, solved[c])

    @pl.when(jnp.logical_and(is_top, odd))
    def _():
        rhs_load.wait()
        make_part()
        inverse_load.wait()
        gram[...] = squared(inverse[...])
        pl.semaphore_wait(barrier, greetings)

        def solve(c):
            up_copy[c].wait_recv()
            solved[c] = product(gram[...], right_operand(rhs[:, spans[c]] - up_in[c]))
            if c == 0:
                pl.semaphore_wait(clear_sem, 1)
            down_copy[c].start()

        pair_copy.wait_recv()
        rise_copy.wait_recv()
        gathered[...] = part[...] + pair_in[...] + rise_in[...]
        for copy in hub_copy:
            copy.start()
        for c in range(chunks - 1):
            solve(c)
        hubs_all.wait_recv()
        value = gathered[...]
        for j in range(hubs - 1):
            value = value + hub_in[j]
        total_in[...] = value
        fall_copy.start()
        mate_copy.start()
        solve(chunks - 1)
        make_factor()
        for c in range(chunks):
            store(c, solved[c])
        hubs_all.wait_send()
        fall_copy.wait_send()
        mate_copy.wait_send()
        all_sent(solved, down_send)

    def make_next():
        matrix = spread_matrix(slots // 2)
        spread_next[...] = left_operand(matrix)

    def make_own():
        matrix = spread_matrix(0)
        spread_own[...] = left_operand(matrix)

    def make_turned():
        for matrix, turned in ((spread_own, turned_own), (spread_next, turned_next)):
            for piece in range(3):
                span = pl.ds(piece * width, width)
                turned[:, span] = matrix[:, span].T

    def take(c):
        value = rhs[:, spans[c]]
        if levels > 2:

            @pl.when(level > 0)
            def _():
                up_copy[c].wait_recv()

            value = value - jnp.where(level > 0, up_in[c], 0.0)
        operands[c] = right_operand(value)

    def make_base():
        gram[...] = squared(inverse[...])
        for c in range(chunks):
            base[c] = product(gram[...], operands[c])

    def send_next(c):
        take(c)
        next_out[c] = product(spread_next[...], operands[c])
        if c == 0:
            make_part()
            pl.semaphore_wait(barrier, greetings)

            @pl.when(even)
            def _():
                pair_copy.start()

        next_copy[c].start()

    def start_up():
        rows_load.wait()
        block_load.wait()
        inverse_load.wait()
        make_next()
        rhs_load.wait()

    def send_side(c):
        if c < detours:

            @pl.when(is_sender)
            def _():
                away_copy[c].start()

            @pl.when(jnp.logical_not(is_sender))
            def _():
                side_copy[c].start()

        else:
            side_copy[c].start()

    def pass_on():
        if detours:

            @pl.when(is_relay)
            def _():
                for c in range(detours):
                    away_copy[c].wait_recv()
                    relay_copy[c].start()

    def hand_down(c, value):
        if levels > 2:

            @pl.when(level > 0)
            def _():
                solved[c] = value
                down_copy[c].start()

    def await_down():
        if levels > 2:

            @pl.when(level > 0)
            def _():
                all_sent(solved, down_send)

    @pl.when(is_host)
    def _():
        start_up()
        for c in range(chunks):
            send_next(c)
        make_own()
        for c in range(chunks):
            own[c] = product(spread_own[...], operands[c])
        make_turned()
        make_base()
        corner_copy.wait_recv()
        packed_copy.wait_recv()
        gram_top[...] = squared(unpack())
        for c in range(chunks):
            next_copy[c].wait_recv()
            give_copy[c].wait_recv()
            operand = right_operand(top_rhs[c] - (own[c] + next_in[c]))
            value = product(gram_top[...], operand)
            own_in[c] = value
            send_side(c)
            lift_copy[c].start()
            base[c] = base[c] - product(turned_own[...], right_operand(value))
        for c in range(chunks):
            if c == chunks - 1:
                mate_copy.wait_recv()
                make_factor()
                for d in range(c):
                    store(d, base[d])
            side_copy[c].wait_recv()
            value = base[c] - product(turned_next[...], right_operand(beside_in[c]))
            hand_down(c, value)
            if c == chunks - 1:
                store(c, value)
            else:
                base[c] = value
        pair_copy.wait_send()
        all_sent(next_out, next_send)
        all_sent(own_in, up_send)
        all_sent(own_in, side_send)
        await_down()

    def climb(leads):
        start_up()
        early = min(2, chunks)
        for c in range(early):
            send_next(c)
        make_own()
        for c in range(early):
            own[c] = product(spread_own[...], operands[c])
        if leads:
            gather_pair()
            rise_copy.start()
        for c in range(early):
            next_copy[c].wait_recv()
            own[c] = own[c] + next_in[c]
            up_copy[c].start()
        for c in range(early, chunks):
            send_next(c)
            own[c] = product(spread_own[...], operands[c])
        for c in range(early, chunks):
            next_copy[c].wait_recv()
            own[c] = own[c] + next_in[c]
            up_copy[c].start()
        make_turned()
        make_base()
        if leads:
            pass_on()

        def spread_total():
            if leads:
                fall_copy.wait_recv()
                mate_copy.start()
                if levels > 2:

                    @pl.when(level > 0)
                    def _():
                        fall_copy.start()

                make_factor()

        def own_part(c):
            down_copy[c].wait_recv()
            send_side(c)
            base[c] = base[c] - product(turned_own[...], right_operand(own_in[c]))

        def beside_part(c, known):
            side_copy[c].wait_recv()
            value = base[c] - product(turned_next[...], right_operand(beside_in[c]))
            hand_down(c, value)
            if leads and known:
                store(c, value)
            else:
                base[c] = value

        for c in range(chunks - 1):
            own_part(c)
            if c > 0:
                beside_part(c, False)
        spread_total()
        if leads:
            for c in range(1, chunks - 1):
                store(c, base[c])
        own_part(chunks - 1)
        for c in (chunks - 1, 0) if chunks > 1 else (0,):
            beside_part(c, True)
        if not leads:
            mate_copy.wait_recv()
            make_factor()
            for c in range(chunks):
                store(c, base[c])
        all_sent(next_out, next_send)
        all_sent(own, up_send)
        all_sent(own_in, side_send)
        if leads and detours:

            @pl.when(is_relay)
            def _():
                all_sent(relayed, relay_send)

        if leads:
            rise_copy.wait_send()
            mate_copy.wait_send()
            if levels > 2:

                @pl.when(level > 0)
                def _():
                    fall_copy.wait_send()
        else:
            pair_copy.wait_send()
        await_down()

    @pl.when(jnp.logical_and(has_up, odd))
    def _():
        climb(True)

    if levels > 2:

        @pl.when(jnp.logical_and(level < levels - 2, even))
        def _():
            climb(False)


def per_device(factor_inv, update_blocks, update_rows, right_side):
    levels = lax.axis_size("level")
    subs = lax.axis_size("sub")
    width = factor_inv.shape[-1]
    columns = right_side.shape[-1]
    slots, block_rows = update_blocks.shape[2:4]
    chunks = columns // LANES
    hubs = subs // 2
    piece = pltpu.VMEM((chunks, width, LANES), jnp.float32)
    wide = pltpu.VMEM((width, 3 * width), jnp.bfloat16)
    line = pltpu.VMEM((1, columns), jnp.float32)
    chunk_sem = pltpu.SemaphoreType.DMA((chunks,))
    in_hbm = pl.BlockSpec(memory_space=pltpu.HBM)
    held = [
        pltpu.with_memory_space_constraint(array, pltpu.HBM)
        for array in (update_rows[0, 0], factor_inv[0, 0], update_blocks[0, 0], right_side[0, 0])
    ]
    value = pl.pallas_call(
        functools.partial(kernel, levels, subs),
        out_shape=jax.ShapeDtypeStruct((width, columns), jnp.float32),
        in_specs=[in_hbm] * 4,
        out_specs=pl.BlockSpec(memory_space=pltpu.VMEM),
        scratch_shapes=[
            pltpu.SMEM((slots,), jnp.int32),
            pltpu.VMEM((width, width), jnp.float32),
            pltpu.VMEM((slots, block_rows, width), jnp.float32),
            pltpu.VMEM((width, columns), jnp.float32),
            pltpu.VMEM((chunks, 3 * width, LANES), jnp.bfloat16),
        ]
        + [wide] * 6
        + [piece] * 7
        + [pltpu.VMEM((min(DETOUR["chunks"], chunks), width, LANES), jnp.float32), piece]
        + [
            pltpu.VMEM((width // 2 + 8, width // 2), jnp.float32),
            pltpu.VMEM((width // 2, width // 2), jnp.float32),
            piece,
        ]
        + [line] * 4
        + [pltpu.VMEM((hubs - 1, 1, columns), jnp.float32)]
        + [line] * 2
        + [pltpu.SemaphoreType.DMA((4,)), pltpu.SemaphoreType.DMA((4,))]
        + [pltpu.SemaphoreType.DMA((2,))]
        + [pltpu.SemaphoreType.DMA, chunk_sem] * 4
        + [pltpu.SemaphoreType.DMA((4,)), pltpu.SemaphoreType.DMA((3,))]
        + [pltpu.SemaphoreType.DMA] * 2
        + [pltpu.SemaphoreType.REGULAR, pltpu.SemaphoreType.DMA]
        + [pltpu.SemaphoreType.DMA((min(DETOUR["chunks"], chunks),))],
        compiler_params=pltpu.CompilerParams(
            collective_id=0, has_side_effects=True, vmem_limit_bytes=32 * 1024 * 1024
        ),
        name="staircase",
    )(*held)
    return value[None, None]


def solution(mesh):
    return jax.shard_map(
        per_device,
        mesh=mesh,
        in_specs=(
            P("level", "sub", None, None),
            P("level", "sub", None, None, None),
            P("level", "sub", None),
            P("level", "sub", None, None),
        ),
        out_specs=P("level", "sub", None, None),
        check_vma=False,
    )
```

```python
import functools

import jax
import jax.numpy as jnp
from jax import lax
from jax.experimental import pallas as pl
from jax.experimental.pallas import tpu as pltpu
from jax.sharding import PartitionSpec as P

LANES = 128
SENDER, RELAYS, RECEIVER = 2, (5, 9), 1
MESH = pl.DeviceIdType.MESH


def halves(value):
    high = value.astype(jnp.bfloat16)
    low = (value - high.astype(jnp.float32)).astype(jnp.bfloat16)
    return high, low


def left_operand(matrix):
    high, low = halves(matrix)
    return jnp.concatenate([high, low, high], axis=1)


def right_operand(values):
    high, low = halves(values)
    return jnp.concatenate([high, high, low], axis=0)


def product(left, right):
    return jnp.dot(left, right, preferred_element_type=jnp.float32)


def kernel(
    levels,
    subs,
    rows_hbm,
    inverse_hbm,
    blocks_hbm,
    rhs_hbm,
    x_ref,
    rows,
    inverse,
    blocks,
    rhs,
    operands,
    forwards,
    inverse_left,
    block_own,
    block_next,
    spread_own,
    spread_next,
    turned_own,
    turned_next,
    gram,
    gram_top,
    base,
    own,
    next_out,
    next_in,
    up_in,
    own_in,
    beside_in,
    relayed,
    solved,
    packed,
    top_corner,
    top_rhs,
    part,
    pair_in,
    rise_in,
    gathered,
    hub_in,
    total_in,
    factor,
    next_send,
    next_recv,
    up_send,
    down_send,
    down_recv,
    side_send,
    side_recv,
    sums_send,
    sums_recv,
    clear_sem,
    relay_recv,
):
    level = lax.axis_index("level")
    sub = lax.axis_index("sub")
    chunks = rhs.shape[1] // LANES
    width = inverse.shape[0]
    half = width // 2
    slots = blocks.shape[0]
    hubs = subs // 2
    right = {"sub": lax.rem(sub + 1, subs)}
    left = {"sub": lax.rem(sub + subs - 1, subs)}
    detour = subs > max(RELAYS)
    share = width // len(RELAYS)
    above = {"level": level + 1}
    below = {"level": level - 1}
    others = [{"sub": lax.rem(sub + 2 * j, subs)} for j in range(1, hubs)]
    even = lax.rem(sub, 2) == 0
    odd = jnp.logical_not(even)
    is_top = level == levels - 1
    has_up = level < levels - 1
    is_host = jnp.logical_and(level == levels - 2, even)

    rows_load = pltpu.make_async_copy(rows_hbm, rows, down_send)
    block_load = pltpu.make_async_copy(blocks_hbm, blocks, up_send)
    inverse_load = pltpu.make_async_copy(inverse_hbm, inverse, sums_send.at[3])
    rhs_load = pltpu.make_async_copy(rhs_hbm, rhs, sums_send.at[2])
    spans = [pl.ds(c * LANES, LANES) for c in range(chunks)]

    barrier = pltpu.get_barrier_semaphore()

    def greet(device):
        pl.semaphore_signal(barrier, inc=1, device_id=device, device_id_type=MESH)

    @pl.when(has_up)
    def _():
        greet(left)
        greet(above)

    @pl.when(jnp.logical_and(has_up, even))
    def _():
        greet(right)

    is_sender = jnp.logical_and(has_up, sub == SENDER)
    is_relay = jnp.logical_and(has_up, sub == RELAYS[0])
    for number in RELAYS[1:]:
        is_relay = jnp.logical_or(is_relay, jnp.logical_and(has_up, sub == number))
    if detour:

        @pl.when(is_relay)
        def _():
            greet({"sub": SENDER})

        @pl.when(jnp.logical_and(has_up, sub == RECEIVER))
        def _():
            for number in RELAYS:
                greet({"sub": number})

    @pl.when(level > 0)
    def _():
        greet(below)

    @pl.when(jnp.logical_and(is_top, even))
    def _():
        greet(right)

    @pl.when(jnp.logical_and(is_top, odd))
    def _():
        greet(left)
        for device in others:
            greet(device)

    greetings = jnp.where(even, 1, jnp.where(is_top, hubs, 2)) + jnp.where(has_up, 1, 0)
    greetings += jnp.where(level > 0, 1, 0)
    if detour:
        greetings += jnp.where(is_sender, len(RELAYS), jnp.where(is_relay, 1, 0))

    inverse_load.start()

    @pl.when(jnp.logical_not(jnp.logical_and(is_top, even)))
    def _():
        rhs_load.start()

    @pl.when(has_up)
    def _():
        rows_load.start()
        block_load.start()

    def remote(source, target, send, recv, device):
        return pltpu.make_async_remote_copy(
            src_ref=source,
            dst_ref=target,
            send_sem=send,
            recv_sem=recv,
            device_id=device,
            device_id_type=MESH,
        )

    def chunk_copies(source, target, send, recv, device, base=0):
        return [
            remote(source.at[c], target.at[c], send, recv.at[base + c], device)
            for c in range(chunks)
        ]

    def all_sent(array, send):
        remote(array, array, send, send, left).wait_send()

    corner_copy = remote(
        inverse_hbm.at[pl.ds(half, half), pl.ds(0, half)],
        top_corner,
        up_send,
        sums_recv.at[0],
        below,
    )
    packed_copy = remote(packed, packed, down_send, sums_recv.at[1], below)
    give_copy = [
        remote(
            rhs_hbm.at[:, spans[c]],
            top_rhs.at[c],
            next_send if c < chunks - 1 else side_send,
            down_recv.at[c],
            below,
        )
        for c in range(chunks)
    ]
    next_copy = chunk_copies(next_out, next_in, next_send, next_recv, right)
    arrival = 0 if levels == 2 else chunks
    up_copy = chunk_copies(own, up_in, up_send, next_recv, above, arrival)
    lift_copy = chunk_copies(own_in, solved, up_send, next_recv, above, arrival)
    down_copy = chunk_copies(solved, own_in, down_send, down_recv, below)
    side_copy = chunk_copies(own_in, beside_in, side_send, side_recv, left)
    away_copy = [
        remote(
            own_in.at[0, pl.ds(i * share, share)],
            relayed,
            side_send,
            relay_recv,
            {"sub": RELAYS[i]},
        )
        for i in range(len(RELAYS))
    ]
    relay_copy = [
        remote(
            relayed,
            beside_in.at[0, pl.ds(i * share, share)],
            sums_send.at[0],
            side_recv.at[0],
            {"sub": RECEIVER},
        )
        for i in range(len(RELAYS))
    ]
    pair_copy = remote(part, pair_in, sums_send.at[0], sums_recv.at[0], right)
    rise_copy = remote(gathered, rise_in, sums_send.at[1], sums_recv.at[1], above)
    fall_copy = remote(total_in, total_in, sums_send.at[2], sums_recv.at[2], below)
    mate_copy = remote(total_in, total_in, sums_send.at[3], sums_recv.at[2], left)
    hub_copy = [
        remote(gathered, hub_in.at[j], side_send, side_recv.at[0], others[j])
        for j in range(hubs - 1)
    ]
    hubs_all = remote(hub_in, hub_in, side_send, side_recv.at[0], left)

    def placed(slot):
        found = jnp.int32(0)
        for k in range(slots):
            found = jnp.where(rows[k] == slot, k, found)
        return blocks[found]

    def picked(first):
        return left_operand(
            jnp.concatenate([placed(first + d) for d in range(slots // 2)], axis=0)
        )

    def squared(matrix):
        return left_operand(product(left_operand(matrix.T), right_operand(matrix)))

    def make_part():
        for span in spans:
            value = rhs[:, span]
            part[:, span] = jnp.sum(value * value, axis=0, keepdims=True)

    def gather_pair():
        pair_copy.wait_recv()
        if levels > 2:

            @pl.when(level > 0)
            def _():
                rise_copy.wait_recv()

            gathered[...] = part[...] + pair_in[...] + jnp.where(level > 0, rise_in[...], 0.0)
        else:
            gathered[...] = part[...] + pair_in[...]

    def make_factor():
        factor[...] = 1.0 / jnp.sqrt(total_in[...] / (levels * subs * width) + 1e-06)

    def store(c, value):
        x_ref[:, spans[c]] = value * factor[:, spans[c]]

    block_row = lax.broadcasted_iota(jnp.int32, (half, half), 0)
    block_column = lax.broadcasted_iota(jnp.int32, (half, half), 1)

    def pack():
        first = inverse[pl.ds(0, half), pl.ds(0, half)]
        second = inverse[pl.ds(half, half), pl.ds(half, half)]
        packed[pl.ds(0, half)] = jnp.where(block_row >= block_column, first, second.T)
        diagonal = jnp.where(block_row == block_column, second, 0.0)
        packed[pl.ds(half, 8)] = jnp.broadcast_to(
            jnp.sum(diagonal, axis=0, keepdims=True), (8, half)
        )

    def unpack():
        both = packed[pl.ds(0, half)]
        diagonal = packed[pl.ds(half, 1)]
        zero = jnp.zeros((half, half), jnp.float32)
        first = jnp.where(block_row >= block_column, both, 0.0)
        second = jnp.where(block_row < block_column, both, 0.0)
        second = jnp.where(block_row == block_column, diagonal, second).T
        upper = jnp.concatenate([first, zero], axis=1)
        lower = jnp.concatenate([top_corner[...], second], axis=1)
        return jnp.concatenate([upper, lower], axis=0)

    @pl.when(jnp.logical_and(is_top, even))
    def _():
        pl.semaphore_wait(barrier, greetings)
        give_copy[0].start()
        corner_copy.start()
        rhs_load.start()
        inverse_load.wait()
        pack()
        packed_copy.start()
        for copy in give_copy[1:]:
            copy.start()
        rhs_load.wait()
        make_part()
        pair_copy.start()
        pair_copy.wait_send()
        corner_copy.wait_send()
        packed_copy.wait_send()
        all_sent(top_rhs.at[pl.ds(0, chunks - 1)], next_send)
        pl.semaphore_signal(clear_sem, inc=1, device_id=right, device_id_type=MESH)
        give_copy[chunks - 1].wait_send()
        mate_copy.wait_recv()
        make_factor()
        for c in range(chunks):
            lift_copy[c].wait_recv()
            store(c, solved[c])

    @pl.when(jnp.logical_and(is_top, odd))
    def _():
        rhs_load.wait()
        make_part()
        inverse_load.wait()
        gram[...] = squared(inverse[...])
        pl.semaphore_wait(barrier, greetings)

        def solve(c):
            up_copy[c].wait_recv()
            solved[c] = product(gram[...], right_operand(rhs[:, spans[c]] - up_in[c]))
            if c == 0:
                pl.semaphore_wait(clear_sem, 1)
            down_copy[c].start()

        pair_copy.wait_recv()
        rise_copy.wait_recv()
        gathered[...] = part[...] + pair_in[...] + rise_in[...]
        for copy in hub_copy:
            copy.start()
        for c in range(chunks - 1):
            solve(c)
        hubs_all.wait_recv()
        value = gathered[...]
        for j in range(hubs - 1):
            value = value + hub_in[j]
        total_in[...] = value
        fall_copy.start()
        mate_copy.start()
        solve(chunks - 1)
        make_factor()
        for c in range(chunks):
            store(c, solved[c])
        hubs_all.wait_send()
        fall_copy.wait_send()
        mate_copy.wait_send()
        all_sent(solved, down_send)

    def make_spread():
        operand = right_operand(inverse[...])
        spread_next[...] = left_operand(product(block_next[...], operand))
        spread_own[...] = left_operand(product(block_own[...], operand))

    def make_turned():
        for matrix, turned in ((spread_own, turned_own), (spread_next, turned_next)):
            for piece in range(3):
                span = pl.ds(piece * width, width)
                turned[:, span] = matrix[:, span].T

    def take(c):
        value = rhs[:, spans[c]]
        if levels > 2:

            @pl.when(level > 0)
            def _():
                up_copy[c].wait_recv()

            value = value - jnp.where(level > 0, up_in[c], 0.0)
        operand = right_operand(value)
        operands[c] = operand
        forwards[c] = right_operand(product(inverse_left[...], operand))

    def make_base():
        gram[...] = squared(inverse[...])
        for c in range(chunks):
            base[c] = product(gram[...], operands[c])

    def send_next(c):
        take(c)
        if c == 0:
            rows_load.wait()
            block_load.wait()
            block_next[...] = picked(slots // 2)
        next_out[c] = product(block_next[...], forwards[c])
        if c == 0:
            make_part()
            pl.semaphore_wait(barrier, greetings)

            @pl.when(even)
            def _():
                pair_copy.start()

        next_copy[c].start()

    def start_up():
        inverse_load.wait()
        inverse_left[...] = left_operand(inverse[...])
        rhs_load.wait()

    def send_side(c):
        if c == 0 and detour:

            @pl.when(is_sender)
            def _():
                for copy in away_copy:
                    copy.start()

            @pl.when(jnp.logical_not(is_sender))
            def _():
                side_copy[c].start()

        else:
            side_copy[c].start()

    def pass_on():
        if detour:

            @pl.when(is_relay)
            def _():
                away_copy[0].wait_recv()

            for i, number in enumerate(RELAYS):

                @pl.when(jnp.logical_and(has_up, sub == number))
                def _():
                    relay_copy[i].start()

    def hand_down(c, value):
        if levels > 2:

            @pl.when(level > 0)
            def _():
                solved[c] = value
                down_copy[c].start()

    def await_down():
        if levels > 2:

            @pl.when(level > 0)
            def _():
                all_sent(solved, down_send)

    @pl.when(is_host)
    def _():
        start_up()
        for c in range(chunks):
            send_next(c)
        block_own[...] = picked(0)
        for c in range(chunks):
            own[c] = product(block_own[...], forwards[c])
        make_spread()
        make_turned()
        make_base()
        corner_copy.wait_recv()
        packed_copy.wait_recv()
        gram_top[...] = squared(unpack())
        for c in range(chunks):
            next_copy[c].wait_recv()
            give_copy[c].wait_recv()
            operand = right_operand(top_rhs[c] - (own[c] + next_in[c]))
            value = product(gram_top[...], operand)
            own_in[c] = value
            send_side(c)
            lift_copy[c].start()
            base[c] = base[c] - product(turned_own[...], right_operand(value))
        for c in range(chunks):
            if c == chunks - 1:
                mate_copy.wait_recv()
                make_factor()
                for d in range(c):
                    store(d, base[d])
            side_copy[c].wait_recv()
            value = base[c] - product(turned_next[...], right_operand(beside_in[c]))
            hand_down(c, value)
            if c == chunks - 1:
                store(c, value)
            else:
                base[c] = value
        pair_copy.wait_send()
        all_sent(next_out, next_send)
        all_sent(own_in, up_send)
        all_sent(own_in, side_send)
        await_down()

    def climb(leads):
        start_up()
        early = min(2, chunks)
        for c in range(early):
            send_next(c)
        block_own[...] = picked(0)
        for c in range(early):
            own[c] = product(block_own[...], forwards[c])
        if leads:
            gather_pair()
            rise_copy.start()
        for c in range(early):
            next_copy[c].wait_recv()
            own[c] = own[c] + next_in[c]
            up_copy[c].start()
        for c in range(early, chunks):
            send_next(c)
            own[c] = product(block_own[...], forwards[c])
        for c in range(early, chunks):
            next_copy[c].wait_recv()
            own[c] = own[c] + next_in[c]
            up_copy[c].start()
        make_spread()
        make_turned()
        make_base()
        if leads:
            pass_on()

        def spread_total():
            if leads:
                fall_copy.wait_recv()
                mate_copy.start()
                if levels > 2:

                    @pl.when(level > 0)
                    def _():
                        fall_copy.start()

                make_factor()

        def own_part(c):
            down_copy[c].wait_recv()
            send_side(c)
            base[c] = base[c] - product(turned_own[...], right_operand(own_in[c]))

        def beside_part(c, known):
            side_copy[c].wait_recv()
            value = base[c] - product(turned_next[...], right_operand(beside_in[c]))
            hand_down(c, value)
            if leads and known:
                store(c, value)
            else:
                base[c] = value

        for c in range(chunks - 1):
            own_part(c)
            if c > 0:
                beside_part(c, False)
        spread_total()
        if leads:
            for c in range(1, chunks - 1):
                store(c, base[c])
        own_part(chunks - 1)
        for c in (0, chunks - 1) if chunks > 1 else (0,):
            beside_part(c, True)
        if not leads:
            mate_copy.wait_recv()
            make_factor()
            for c in range(chunks):
                store(c, base[c])
        all_sent(next_out, next_send)
        all_sent(own, up_send)
        all_sent(own_in, side_send)
        if leads and detour:

            @pl.when(is_relay)
            def _():
                all_sent(relayed, sums_send.at[0])

        if leads:
            rise_copy.wait_send()
            mate_copy.wait_send()
            if levels > 2:

                @pl.when(level > 0)
                def _():
                    fall_copy.wait_send()
        else:
            pair_copy.wait_send()
        await_down()

    @pl.when(jnp.logical_and(has_up, odd))
    def _():
        climb(True)

    if levels > 2:

        @pl.when(jnp.logical_and(level < levels - 2, even))
        def _():
            climb(False)


def per_device(factor_inv, update_blocks, update_rows, right_side):
    levels = lax.axis_size("level")
    subs = lax.axis_size("sub")
    width = factor_inv.shape[-1]
    columns = right_side.shape[-1]
    slots, block_rows = update_blocks.shape[2:4]
    chunks = columns // LANES
    hubs = subs // 2
    piece = pltpu.VMEM((chunks, width, LANES), jnp.float32)
    wide = pltpu.VMEM((width, 3 * width), jnp.bfloat16)
    line = pltpu.VMEM((1, columns), jnp.float32)
    chunk_sem = pltpu.SemaphoreType.DMA((chunks,))
    in_hbm = pl.BlockSpec(memory_space=pltpu.HBM)
    held = [
        pltpu.with_memory_space_constraint(array, pltpu.HBM)
        for array in (update_rows[0, 0], factor_inv[0, 0], update_blocks[0, 0], right_side[0, 0])
    ]
    value = pl.pallas_call(
        functools.partial(kernel, levels, subs),
        out_shape=jax.ShapeDtypeStruct((width, columns), jnp.float32),
        in_specs=[in_hbm] * 4,
        out_specs=pl.BlockSpec(memory_space=pltpu.VMEM),
        scratch_shapes=[
            pltpu.SMEM((slots,), jnp.int32),
            pltpu.VMEM((width, width), jnp.float32),
            pltpu.VMEM((slots, block_rows, width), jnp.float32),
            pltpu.VMEM((width, columns), jnp.float32),
            pltpu.VMEM((chunks, 3 * width, LANES), jnp.bfloat16),
            pltpu.VMEM((chunks, 3 * width, LANES), jnp.bfloat16),
        ]
        + [wide] * 9
        + [piece] * 7
        + [pltpu.VMEM((width // len(RELAYS), LANES), jnp.float32), piece]
        + [
            pltpu.VMEM((width // 2 + 8, width // 2), jnp.float32),
            pltpu.VMEM((width // 2, width // 2), jnp.float32),
            piece,
        ]
        + [line] * 4
        + [pltpu.VMEM((hubs - 1, 1, columns), jnp.float32)]
        + [line] * 2
        + [pltpu.SemaphoreType.DMA]
        + [pltpu.SemaphoreType.DMA((chunks if levels == 2 else 2 * chunks,))]
        + [pltpu.SemaphoreType.DMA]
        + [pltpu.SemaphoreType.DMA, chunk_sem] * 2
        + [pltpu.SemaphoreType.DMA((4,)), pltpu.SemaphoreType.DMA((3,))]
        + [pltpu.SemaphoreType.REGULAR]
        + [pltpu.SemaphoreType.DMA],
        compiler_params=pltpu.CompilerParams(
            collective_id=0, has_side_effects=True, vmem_limit_bytes=32 * 1024 * 1024
        ),
        name="staircase",
    )(*held)
    return value[None, None]


def solution(mesh):
    return jax.shard_map(
        per_device,
        mesh=mesh,
        in_specs=(
            P("level", "sub", None, None),
            P("level", "sub", None, None, None),
            P("level", "sub", None),
            P("level", "sub", None, None),
        ),
        out_specs=P("level", "sub", None, None),
        check_vma=False,
    )
```

```python
import functools

import jax
import jax.numpy as jnp
from jax import lax
from jax.experimental import pallas as pl
from jax.experimental.pallas import tpu as pltpu
from jax.sharding import PartitionSpec as P

LANES = 128
SENDER, RELAYS, RECEIVER = 2, (5, 9), 1
TAIL_ROWS = 64
MESH = pl.DeviceIdType.MESH


def halves(value):
    high = value.astype(jnp.bfloat16)
    low = (value - high.astype(jnp.float32)).astype(jnp.bfloat16)
    return high, low


def left_operand(matrix):
    high, low = halves(matrix)
    return jnp.concatenate([high, low, high], axis=1)


def right_operand(values):
    high, low = halves(values)
    return jnp.concatenate([high, high, low], axis=0)


def product(left, right):
    return jnp.dot(left, right, preferred_element_type=jnp.float32)


def kernel(
    levels,
    subs,
    rows_hbm,
    inverse_hbm,
    blocks_hbm,
    rhs_hbm,
    x_ref,
    rows,
    inverse,
    blocks,
    rhs,
    operands,
    forwards,
    inverse_left,
    block_own,
    block_next,
    spread_own,
    spread_next,
    turned_own,
    turned_next,
    gram,
    gram_top,
    base,
    own,
    next_out,
    next_in,
    up_in,
    own_in,
    beside_in,
    relayed,
    solved,
    packed,
    top_corner,
    top_rhs,
    part,
    pair_in,
    rise_in,
    gathered,
    hub_in,
    total_in,
    factor,
    next_send,
    next_recv,
    up_send,
    down_send,
    down_recv,
    side_send,
    side_recv,
    sums_send,
    sums_recv,
    clear_sem,
    relay_recv,
):
    level = lax.axis_index("level")
    sub = lax.axis_index("sub")
    chunks = rhs.shape[1] // LANES
    width = inverse.shape[0]
    half = width // 2
    slots = blocks.shape[0]
    hubs = subs // 2
    right = {"sub": lax.rem(sub + 1, subs)}
    left = {"sub": lax.rem(sub + subs - 1, subs)}
    detour = subs > max(RELAYS)
    share = width // len(RELAYS)
    above = {"level": level + 1}
    below = {"level": level - 1}
    others = [{"sub": lax.rem(sub + 2 * j, subs)} for j in range(1, hubs)]
    even = lax.rem(sub, 2) == 0
    odd = jnp.logical_not(even)
    is_top = level == levels - 1
    has_up = level < levels - 1
    is_host = jnp.logical_and(level == levels - 2, even)

    rows_load = pltpu.make_async_copy(rows_hbm, rows, down_send)
    block_load = pltpu.make_async_copy(blocks_hbm, blocks, up_send)
    inverse_load = pltpu.make_async_copy(inverse_hbm, inverse, sums_send.at[3])
    rhs_load = pltpu.make_async_copy(rhs_hbm, rhs, sums_send.at[2])
    spans = [pl.ds(c * LANES, LANES) for c in range(chunks)]

    barrier = pltpu.get_barrier_semaphore()

    def greet(device):
        pl.semaphore_signal(barrier, inc=1, device_id=device, device_id_type=MESH)

    @pl.when(has_up)
    def _():
        greet(left)
        greet(above)

    @pl.when(jnp.logical_and(has_up, even))
    def _():
        greet(right)

    is_sender = jnp.logical_and(has_up, sub == SENDER)
    is_relay = jnp.logical_and(has_up, sub == RELAYS[0])
    for number in RELAYS[1:]:
        is_relay = jnp.logical_or(is_relay, jnp.logical_and(has_up, sub == number))
    if detour:

        @pl.when(is_relay)
        def _():
            greet({"sub": SENDER})

        @pl.when(jnp.logical_and(has_up, sub == RECEIVER))
        def _():
            for number in RELAYS:
                greet({"sub": number})

    @pl.when(level > 0)
    def _():
        greet(below)

    @pl.when(jnp.logical_and(is_top, even))
    def _():
        greet(right)

    @pl.when(jnp.logical_and(is_top, odd))
    def _():
        greet(left)
        for device in others:
            greet(device)

    greetings = jnp.where(even, 1, jnp.where(is_top, hubs, 2)) + jnp.where(has_up, 1, 0)
    greetings += jnp.where(level > 0, 1, 0)
    if detour:
        greetings += jnp.where(is_sender, len(RELAYS), jnp.where(is_relay, 1, 0))

    inverse_load.start()

    @pl.when(jnp.logical_not(jnp.logical_and(is_top, even)))
    def _():
        rhs_load.start()

    @pl.when(has_up)
    def _():
        rows_load.start()
        block_load.start()

    def remote(source, target, send, recv, device):
        return pltpu.make_async_remote_copy(
            src_ref=source,
            dst_ref=target,
            send_sem=send,
            recv_sem=recv,
            device_id=device,
            device_id_type=MESH,
        )

    def chunk_copies(source, target, send, recv, device, base=0):
        return [
            remote(source.at[c], target.at[c], send, recv.at[base + c], device)
            for c in range(chunks)
        ]

    def all_sent(array, send):
        remote(array, array, send, send, left).wait_send()

    corner_copy = remote(
        inverse_hbm.at[pl.ds(half, half), pl.ds(0, half)],
        top_corner,
        up_send,
        sums_recv.at[0],
        below,
    )
    packed_copy = remote(packed, packed, down_send, sums_recv.at[1], below)
    give_copy = [
        remote(
            rhs_hbm.at[:, spans[c]],
            top_rhs.at[c],
            next_send if c < chunks - 1 else side_send,
            down_recv.at[c],
            below,
        )
        for c in range(chunks)
    ]
    next_copy = chunk_copies(next_out, next_in, next_send, next_recv, right)
    arrival = 0 if levels == 2 else chunks
    up_copy = chunk_copies(own, up_in, up_send, next_recv, above, arrival)
    lift_copy = chunk_copies(own_in, solved, up_send, next_recv, above, arrival)
    down_copy = chunk_copies(solved, own_in, down_send, down_recv, below)
    side_copy = chunk_copies(own_in, beside_in, side_send, side_recv, left)
    away_copy = [
        remote(
            own_in.at[0, pl.ds(i * share, share)],
            relayed,
            side_send,
            relay_recv,
            {"sub": RELAYS[i]},
        )
        for i in range(len(RELAYS))
    ]
    relay_copy = [
        remote(
            relayed,
            beside_in.at[0, pl.ds(i * share, share)],
            sums_send.at[0],
            side_recv.at[0],
            {"sub": RECEIVER},
        )
        for i in range(len(RELAYS))
    ]
    split = levels == 2 and chunks > 1 and TAIL_ROWS % chunks == 0
    final = chunks - 1
    body = width - TAIL_ROWS
    body_rows, tail_rows = pl.ds(0, body), pl.ds(body, TAIL_ROWS)
    body_down = remote(
        solved.at[final, body_rows],
        own_in.at[final, body_rows],
        down_send,
        down_recv.at[final],
        below,
    )
    tail_down = remote(
        solved.at[final, tail_rows],
        own_in.at[final, tail_rows],
        down_send,
        sums_recv.at[1],
        below,
    )
    tail_across = remote(
        solved.at[final, tail_rows],
        beside_in.at[final, tail_rows],
        sums_send.at[0],
        side_recv.at[final],
        {"level": level - 1, "sub": lax.rem(sub + subs - 1, subs)},
    )
    body_side = remote(
        own_in.at[final, body_rows],
        beside_in.at[final, body_rows],
        side_send,
        side_recv.at[final],
        left,
    )
    pair_copy = remote(part, pair_in, sums_send.at[0], sums_recv.at[0], right)
    rise_copy = remote(gathered, rise_in, sums_send.at[1], sums_recv.at[1], above)
    fall_copy = remote(total_in, total_in, sums_send.at[2], sums_recv.at[2], below)
    mate_copy = remote(total_in, total_in, sums_send.at[3], sums_recv.at[2], left)
    hub_copy = [
        remote(gathered, hub_in.at[j], side_send, side_recv.at[0], others[j])
        for j in range(hubs - 1)
    ]
    hubs_all = remote(hub_in, hub_in, side_send, side_recv.at[0], left)

    def placed(slot):
        found = jnp.int32(0)
        for k in range(slots):
            found = jnp.where(rows[k] == slot, k, found)
        return blocks[found]

    def picked(first):
        return left_operand(
            jnp.concatenate([placed(first + d) for d in range(slots // 2)], axis=0)
        )

    def squared(matrix):
        return left_operand(product(left_operand(matrix.T), right_operand(matrix)))

    def make_part():
        for span in spans:
            value = rhs[:, span]
            part[:, span] = jnp.sum(value * value, axis=0, keepdims=True)

    def gather_pair():
        pair_copy.wait_recv()
        if levels > 2:

            @pl.when(level > 0)
            def _():
                rise_copy.wait_recv()

            gathered[...] = part[...] + pair_in[...] + jnp.where(level > 0, rise_in[...], 0.0)
        else:
            gathered[...] = part[...] + pair_in[...]

    def make_factor():
        factor[...] = 1.0 / jnp.sqrt(total_in[...] / (levels * subs * width) + 1e-06)

    def store(c, value):
        x_ref[:, spans[c]] = value * factor[:, spans[c]]

    block_row = lax.broadcasted_iota(jnp.int32, (half, half), 0)
    block_column = lax.broadcasted_iota(jnp.int32, (half, half), 1)

    def pack():
        first = inverse[pl.ds(0, half), pl.ds(0, half)]
        second = inverse[pl.ds(half, half), pl.ds(half, half)]
        packed[pl.ds(0, half)] = jnp.where(block_row >= block_column, first, second.T)
        diagonal = jnp.where(block_row == block_column, second, 0.0)
        packed[pl.ds(half, 8)] = jnp.broadcast_to(
            jnp.sum(diagonal, axis=0, keepdims=True), (8, half)
        )

    def unpack():
        both = packed[pl.ds(0, half)]
        diagonal = packed[pl.ds(half, 1)]
        zero = jnp.zeros((half, half), jnp.float32)
        first = jnp.where(block_row >= block_column, both, 0.0)
        second = jnp.where(block_row < block_column, both, 0.0)
        second = jnp.where(block_row == block_column, diagonal, second).T
        upper = jnp.concatenate([first, zero], axis=1)
        lower = jnp.concatenate([top_corner[...], second], axis=1)
        return jnp.concatenate([upper, lower], axis=0)

    @pl.when(jnp.logical_and(is_top, even))
    def _():
        pl.semaphore_wait(barrier, greetings)
        give_copy[0].start()
        corner_copy.start()
        rhs_load.start()
        inverse_load.wait()
        pack()
        packed_copy.start()
        for copy in give_copy[1:]:
            copy.start()
        rhs_load.wait()
        make_part()
        pair_copy.start()
        pair_copy.wait_send()
        corner_copy.wait_send()
        packed_copy.wait_send()
        all_sent(top_rhs.at[pl.ds(0, chunks - 1)], next_send)
        pl.semaphore_signal(clear_sem, inc=1, device_id=right, device_id_type=MESH)
        give_copy[chunks - 1].wait_send()
        mate_copy.wait_recv()
        make_factor()
        for c in range(chunks):
            lift_copy[c].wait_recv()
            store(c, solved[c])

    @pl.when(jnp.logical_and(is_top, odd))
    def _():
        rhs_load.wait()
        make_part()
        inverse_load.wait()
        gram[...] = squared(inverse[...])
        pl.semaphore_wait(barrier, greetings)

        def solve(c):
            up_copy[c].wait_recv()
            solved[c] = product(gram[...], right_operand(rhs[:, spans[c]] - up_in[c]))
            if c == 0:
                pl.semaphore_wait(clear_sem, 1)
            if split and c == final:
                body_down.start()
                tail_across.start()
                tail_down.start()
            else:
                down_copy[c].start()

        pair_copy.wait_recv()
        rise_copy.wait_recv()
        gathered[...] = part[...] + pair_in[...] + rise_in[...]
        for copy in hub_copy:
            copy.start()
        for c in range(chunks - 1):
            solve(c)
        hubs_all.wait_recv()
        value = gathered[...]
        for j in range(hubs - 1):
            value = value + hub_in[j]
        total_in[...] = value
        fall_copy.start()
        mate_copy.start()
        solve(chunks - 1)
        make_factor()
        for c in range(chunks):
            store(c, solved[c])
        hubs_all.wait_send()
        fall_copy.wait_send()
        mate_copy.wait_send()
        if split:
            tail_across.wait_send()
        all_sent(solved, down_send)

    def make_spread():
        operand = right_operand(inverse[...])
        spread_next[...] = left_operand(product(block_next[...], operand))
        spread_own[...] = left_operand(product(block_own[...], operand))

    def make_turned():
        for matrix, turned in ((spread_own, turned_own), (spread_next, turned_next)):
            for piece in range(3):
                span = pl.ds(piece * width, width)
                turned[:, span] = matrix[:, span].T

    def take(c):
        value = rhs[:, spans[c]]
        if levels > 2:

            @pl.when(level > 0)
            def _():
                up_copy[c].wait_recv()

            value = value - jnp.where(level > 0, up_in[c], 0.0)
        operand = right_operand(value)
        operands[c] = operand
        forwards[c] = right_operand(product(inverse_left[...], operand))

    def make_base():
        gram[...] = squared(inverse[...])
        for c in range(chunks):
            base[c] = product(gram[...], operands[c])

    def send_next(c):
        take(c)
        if c == 0:
            rows_load.wait()
            block_load.wait()
            block_next[...] = picked(slots // 2)
        next_out[c] = product(block_next[...], forwards[c])
        if c == 0:
            make_part()
            pl.semaphore_wait(barrier, greetings)

            @pl.when(even)
            def _():
                pair_copy.start()

        next_copy[c].start()

    def start_up():
        inverse_load.wait()
        inverse_left[...] = left_operand(inverse[...])
        rhs_load.wait()

    def send_side(c):
        if c == 0 and detour:

            @pl.when(is_sender)
            def _():
                for copy in away_copy:
                    copy.start()

            @pl.when(jnp.logical_not(is_sender))
            def _():
                side_copy[c].start()

        else:
            side_copy[c].start()

    def pass_on():
        if detour:

            @pl.when(is_relay)
            def _():
                away_copy[0].wait_recv()

            for i, number in enumerate(RELAYS):

                @pl.when(jnp.logical_and(has_up, sub == number))
                def _():
                    relay_copy[i].start()

    def hand_down(c, value):
        if levels > 2:

            @pl.when(level > 0)
            def _():
                solved[c] = value
                down_copy[c].start()

    def await_down():
        if levels > 2:

            @pl.when(level > 0)
            def _():
                all_sent(solved, down_send)

    @pl.when(is_host)
    def _():
        start_up()
        for c in range(chunks):
            send_next(c)
        block_own[...] = picked(0)
        for c in range(chunks):
            own[c] = product(block_own[...], forwards[c])
        make_spread()
        make_turned()
        make_base()
        corner_copy.wait_recv()
        packed_copy.wait_recv()
        gram_top[...] = squared(unpack())
        for c in range(chunks):
            next_copy[c].wait_recv()
            give_copy[c].wait_recv()
            operand = right_operand(top_rhs[c] - (own[c] + next_in[c]))
            value = product(gram_top[...], operand)
            own_in[c] = value
            send_side(c)
            lift_copy[c].start()
            base[c] = base[c] - product(turned_own[...], right_operand(value))
        for c in range(chunks):
            if c == chunks - 1:
                mate_copy.wait_recv()
                make_factor()
                for d in range(c):
                    store(d, base[d])
            side_copy[c].wait_recv()
            value = base[c] - product(turned_next[...], right_operand(beside_in[c]))
            hand_down(c, value)
            if c == chunks - 1:
                store(c, value)
            else:
                base[c] = value
        pair_copy.wait_send()
        all_sent(next_out, next_send)
        all_sent(own_in, up_send)
        all_sent(own_in, side_send)
        await_down()

    def climb(leads):
        start_up()
        early = min(2, chunks)
        for c in range(early):
            send_next(c)
        block_own[...] = picked(0)
        for c in range(early):
            own[c] = product(block_own[...], forwards[c])
        if leads:
            gather_pair()
            rise_copy.start()
        for c in range(early):
            next_copy[c].wait_recv()
            own[c] = own[c] + next_in[c]
            up_copy[c].start()
        for c in range(early, chunks):
            send_next(c)
            own[c] = product(block_own[...], forwards[c])
        for c in range(early, chunks):
            next_copy[c].wait_recv()
            own[c] = own[c] + next_in[c]
            up_copy[c].start()
        make_spread()
        make_turned()
        make_base()
        if leads:
            pass_on()

        def spread_total():
            if leads:
                fall_copy.wait_recv()
                mate_copy.start()
                if levels > 2:

                    @pl.when(level > 0)
                    def _():
                        fall_copy.start()

                make_factor()

        def take_down(c):
            if split and leads and c == final:
                body_down.wait_recv()
                body_side.start()
            else:
                down_copy[c].wait_recv()
                send_side(c)

        def own_part(c):
            if split and leads and c == final:
                tail_down.wait_recv()
            base[c] = base[c] - product(turned_own[...], right_operand(own_in[c]))

        def beside_part(c, known):
            side_copy[c].wait_recv()
            value = base[c] - product(turned_next[...], right_operand(beside_in[c]))
            hand_down(c, value)
            if leads and known:
                store(c, value)
            else:
                base[c] = value

        for c in range(final):
            take_down(c)
            own_part(c)
            if c > 0:
                beside_part(c, False)
        spread_total()
        if leads:
            for c in range(1, final):
                store(c, base[c])
        take_down(final)
        own_part(final)
        if final > 0:
            beside_part(0, True)
        beside_part(final, True)
        if not leads:
            mate_copy.wait_recv()
            make_factor()
            for c in range(chunks):
                store(c, base[c])
        all_sent(next_out, next_send)
        all_sent(own, up_send)
        if split and leads:
            all_sent(own_in.at[:, pl.ds(0, width - TAIL_ROWS // chunks)], side_send)
        else:
            all_sent(own_in, side_send)
        if leads and detour:

            @pl.when(is_relay)
            def _():
                all_sent(relayed, sums_send.at[0])

        if leads:
            rise_copy.wait_send()
            mate_copy.wait_send()
            if levels > 2:

                @pl.when(level > 0)
                def _():
                    fall_copy.wait_send()
        else:
            pair_copy.wait_send()
        await_down()

    @pl.when(jnp.logical_and(has_up, odd))
    def _():
        climb(True)

    if levels > 2:

        @pl.when(jnp.logical_and(level < levels - 2, even))
        def _():
            climb(False)


def per_device(factor_inv, update_blocks, update_rows, right_side):
    levels = lax.axis_size("level")
    subs = lax.axis_size("sub")
    width = factor_inv.shape[-1]
    columns = right_side.shape[-1]
    slots, block_rows = update_blocks.shape[2:4]
    chunks = columns // LANES
    hubs = subs // 2
    piece = pltpu.VMEM((chunks, width, LANES), jnp.float32)
    wide = pltpu.VMEM((width, 3 * width), jnp.bfloat16)
    line = pltpu.VMEM((1, columns), jnp.float32)
    chunk_sem = pltpu.SemaphoreType.DMA((chunks,))
    in_hbm = pl.BlockSpec(memory_space=pltpu.HBM)
    held = [
        pltpu.with_memory_space_constraint(array, pltpu.HBM)
        for array in (update_rows[0, 0], factor_inv[0, 0], update_blocks[0, 0], right_side[0, 0])
    ]
    value = pl.pallas_call(
        functools.partial(kernel, levels, subs),
        out_shape=jax.ShapeDtypeStruct((width, columns), jnp.float32),
        in_specs=[in_hbm] * 4,
        out_specs=pl.BlockSpec(memory_space=pltpu.VMEM),
        scratch_shapes=[
            pltpu.SMEM((slots,), jnp.int32),
            pltpu.VMEM((width, width), jnp.float32),
            pltpu.VMEM((slots, block_rows, width), jnp.float32),
            pltpu.VMEM((width, columns), jnp.float32),
            pltpu.VMEM((chunks, 3 * width, LANES), jnp.bfloat16),
            pltpu.VMEM((chunks, 3 * width, LANES), jnp.bfloat16),
        ]
        + [wide] * 9
        + [piece] * 7
        + [pltpu.VMEM((width // len(RELAYS), LANES), jnp.float32), piece]
        + [
            pltpu.VMEM((width // 2 + 8, width // 2), jnp.float32),
            pltpu.VMEM((width // 2, width // 2), jnp.float32),
            piece,
        ]
        + [line] * 4
        + [pltpu.VMEM((hubs - 1, 1, columns), jnp.float32)]
        + [line] * 2
        + [pltpu.SemaphoreType.DMA]
        + [pltpu.SemaphoreType.DMA((chunks if levels == 2 else 2 * chunks,))]
        + [pltpu.SemaphoreType.DMA]
        + [pltpu.SemaphoreType.DMA, chunk_sem] * 2
        + [pltpu.SemaphoreType.DMA((4,)), pltpu.SemaphoreType.DMA((3,))]
        + [pltpu.SemaphoreType.REGULAR]
        + [pltpu.SemaphoreType.DMA],
        compiler_params=pltpu.CompilerParams(
            collective_id=0, has_side_effects=True, vmem_limit_bytes=32 * 1024 * 1024
        ),
        name="staircase",
    )(*held)
    return value[None, None]


def solution(mesh):
    return jax.shard_map(
        per_device,
        mesh=mesh,
        in_specs=(
            P("level", "sub", None, None),
            P("level", "sub", None, None, None),
            P("level", "sub", None),
            P("level", "sub", None, None),
        ),
        out_specs=P("level", "sub", None, None),
        check_vma=False,
    )
```

```python
import functools

import jax
import jax.numpy as jnp
from jax import lax
from jax.experimental import pallas as pl
from jax.experimental.pallas import tpu as pltpu
from jax.sharding import PartitionSpec as P

LANES = 128
SENDER, RELAYS, RECEIVER = 2, (5, 9), 1
TAIL_ROWS = 64
MESH = pl.DeviceIdType.MESH


def halves(value):
    high = value.astype(jnp.bfloat16)
    low = (value - high.astype(jnp.float32)).astype(jnp.bfloat16)
    return high, low


def left_operand(matrix):
    high, low = halves(matrix)
    return jnp.concatenate([high, low], axis=1)


def right_operand(values):
    high, low = halves(values)
    return jnp.concatenate([high, low], axis=1)


def product(left, right):
    depth, columns = right.shape[0], right.shape[1] // 2
    upper = jnp.dot(left[:, :depth], right, preferred_element_type=jnp.float32)
    lower = jnp.dot(left[:, depth:], right[:, :columns], preferred_element_type=jnp.float32)
    return upper[:, :columns] + (upper[:, columns:] + lower)


def kernel(
    levels,
    subs,
    rows_hbm,
    inverse_hbm,
    blocks_hbm,
    rhs_hbm,
    x_ref,
    rows,
    inverse,
    blocks,
    rhs,
    operands,
    forwards,
    inverse_left,
    block_own,
    block_next,
    spread_own,
    spread_next,
    turned_own,
    turned_next,
    gram,
    gram_top,
    base,
    own,
    next_out,
    next_in,
    up_in,
    own_in,
    beside_in,
    relayed,
    solved,
    packed,
    top_corner,
    top_rhs,
    part,
    pair_in,
    rise_in,
    gathered,
    hub_in,
    total_in,
    factor,
    next_send,
    next_recv,
    up_send,
    down_send,
    down_recv,
    side_send,
    side_recv,
    sums_send,
    sums_recv,
    clear_sem,
    relay_recv,
):
    level = lax.axis_index("level")
    sub = lax.axis_index("sub")
    chunks = rhs.shape[1] // LANES
    width = inverse.shape[0]
    half = width // 2
    slots = blocks.shape[0]
    hubs = subs // 2
    right = {"sub": lax.rem(sub + 1, subs)}
    left = {"sub": lax.rem(sub + subs - 1, subs)}
    detour = subs > max(RELAYS)
    share = width // len(RELAYS)
    above = {"level": level + 1}
    below = {"level": level - 1}
    others = [{"sub": lax.rem(sub + 2 * j, subs)} for j in range(1, hubs)]
    even = lax.rem(sub, 2) == 0
    odd = jnp.logical_not(even)
    is_top = level == levels - 1
    has_up = level < levels - 1
    is_host = jnp.logical_and(level == levels - 2, even)

    rows_load = pltpu.make_async_copy(rows_hbm, rows, down_send)
    block_load = pltpu.make_async_copy(blocks_hbm, blocks, up_send)
    inverse_load = pltpu.make_async_copy(inverse_hbm, inverse, sums_send.at[3])
    head, rest = pl.ds(0, LANES), pl.ds(LANES, rhs.shape[1] - LANES)
    head_load = pltpu.make_async_copy(rhs_hbm.at[:, head], rhs.at[:, head], sums_send.at[1])
    rest_load = pltpu.make_async_copy(rhs_hbm.at[:, rest], rhs.at[:, rest], sums_send.at[2])
    rhs_load = pltpu.make_async_copy(rhs_hbm, rhs, sums_send.at[2])
    spans = [pl.ds(c * LANES, LANES) for c in range(chunks)]

    barrier = pltpu.get_barrier_semaphore()

    def greet(device):
        pl.semaphore_signal(barrier, inc=1, device_id=device, device_id_type=MESH)

    @pl.when(has_up)
    def _():
        greet(left)
        greet(above)

    @pl.when(jnp.logical_and(has_up, even))
    def _():
        greet(right)

    is_sender = jnp.logical_and(has_up, sub == SENDER)
    is_relay = jnp.logical_and(has_up, sub == RELAYS[0])
    for number in RELAYS[1:]:
        is_relay = jnp.logical_or(is_relay, jnp.logical_and(has_up, sub == number))
    if detour:

        @pl.when(is_relay)
        def _():
            greet({"sub": SENDER})

        @pl.when(jnp.logical_and(has_up, sub == RECEIVER))
        def _():
            for number in RELAYS:
                greet({"sub": number})

    @pl.when(level > 0)
    def _():
        greet(below)

    @pl.when(jnp.logical_and(is_top, even))
    def _():
        greet(right)

    @pl.when(jnp.logical_and(is_top, odd))
    def _():
        greet(left)
        for device in others:
            greet(device)

    greetings = jnp.where(even, 1, jnp.where(is_top, hubs, 2)) + jnp.where(has_up, 1, 0)
    greetings += jnp.where(level > 0, 1, 0)
    if detour:
        greetings += jnp.where(is_sender, len(RELAYS), jnp.where(is_relay, 1, 0))

    inverse_load.start()

    @pl.when(jnp.logical_and(is_top, odd))
    def _():
        rhs_load.start()

    @pl.when(has_up)
    def _():
        head_load.start()
        rows_load.start()
        block_load.start()
        rest_load.start()

    def remote(source, target, send, recv, device):
        return pltpu.make_async_remote_copy(
            src_ref=source,
            dst_ref=target,
            send_sem=send,
            recv_sem=recv,
            device_id=device,
            device_id_type=MESH,
        )

    def chunk_copies(source, target, send, recv, device, base=0):
        return [
            remote(source.at[c], target.at[c], send, recv.at[base + c], device)
            for c in range(chunks)
        ]

    def all_sent(array, send):
        remote(array, array, send, send, left).wait_send()

    corner_copy = remote(
        inverse_hbm.at[pl.ds(half, half), pl.ds(0, half)],
        top_corner,
        up_send,
        sums_recv.at[0],
        below,
    )
    packed_copy = remote(packed, packed, down_send, sums_recv.at[1], below)
    give_copy = [
        remote(
            rhs_hbm.at[:, spans[c]],
            top_rhs.at[c],
            next_send if c < chunks - 1 else side_send,
            down_recv.at[c],
            below,
        )
        for c in range(chunks)
    ]
    next_copy = chunk_copies(next_out, next_in, next_send, next_recv, right)
    arrival = 0 if levels == 2 else chunks
    up_copy = chunk_copies(own, up_in, up_send, next_recv, above, arrival)
    lift_copy = chunk_copies(own_in, solved, up_send, next_recv, above, arrival)
    down_copy = chunk_copies(solved, own_in, down_send, down_recv, below)
    side_copy = chunk_copies(own_in, beside_in, side_send, side_recv, left)
    away_copy = [
        remote(
            own_in.at[0, pl.ds(i * share, share)],
            relayed,
            side_send,
            relay_recv,
            {"sub": RELAYS[i]},
        )
        for i in range(len(RELAYS))
    ]
    relay_copy = [
        remote(
            relayed,
            beside_in.at[0, pl.ds(i * share, share)],
            sums_send.at[0],
            side_recv.at[0],
            {"sub": RECEIVER},
        )
        for i in range(len(RELAYS))
    ]
    split = levels == 2 and chunks > 1 and TAIL_ROWS % chunks == 0
    final = chunks - 1
    body = width - TAIL_ROWS
    body_rows, tail_rows = pl.ds(0, body), pl.ds(body, TAIL_ROWS)
    body_down = remote(
        solved.at[final, body_rows],
        own_in.at[final, body_rows],
        down_send,
        down_recv.at[final],
        below,
    )
    tail_down = remote(
        solved.at[final, tail_rows],
        own_in.at[final, tail_rows],
        down_send,
        sums_recv.at[1],
        below,
    )
    tail_across = remote(
        solved.at[final, tail_rows],
        beside_in.at[final, tail_rows],
        sums_send.at[0],
        side_recv.at[final],
        {"level": level - 1, "sub": lax.rem(sub + subs - 1, subs)},
    )
    body_side = remote(
        own_in.at[final, body_rows],
        beside_in.at[final, body_rows],
        side_send,
        side_recv.at[final],
        left,
    )
    pair_copy = remote(part, pair_in, sums_send.at[0], sums_recv.at[0], right)
    rise_copy = remote(gathered, rise_in, sums_send.at[1], sums_recv.at[1], above)
    fall_copy = remote(total_in, total_in, sums_send.at[2], sums_recv.at[2], below)
    mate_copy = remote(total_in, total_in, sums_send.at[3], sums_recv.at[2], left)
    hub_copy = [
        remote(gathered, hub_in.at[j], side_send, side_recv.at[0], others[j])
        for j in range(hubs - 1)
    ]
    hubs_all = remote(hub_in, hub_in, side_send, side_recv.at[0], left)

    def placed(slot):
        found = jnp.int32(0)
        for k in range(slots):
            found = jnp.where(rows[k] == slot, k, found)
        return blocks[found]

    def picked(first):
        return left_operand(
            jnp.concatenate([placed(first + d) for d in range(slots // 2)], axis=0)
        )

    def squared(matrix):
        return left_operand(product(left_operand(matrix.T), right_operand(matrix)))

    def make_part():
        for span in spans:
            value = rhs[:, span]
            part[:, span] = jnp.sum(value * value, axis=0, keepdims=True)

    def gather_pair():
        pair_copy.wait_recv()
        if levels > 2:

            @pl.when(level > 0)
            def _():
                rise_copy.wait_recv()

            gathered[...] = part[...] + pair_in[...] + jnp.where(level > 0, rise_in[...], 0.0)
        else:
            gathered[...] = part[...] + pair_in[...]

    def make_factor():
        factor[...] = 1.0 / jnp.sqrt(total_in[...] / (levels * subs * width) + 1e-06)

    def store(c, value):
        x_ref[:, spans[c]] = value * factor[:, spans[c]]

    block_row = lax.broadcasted_iota(jnp.int32, (half, half), 0)
    block_column = lax.broadcasted_iota(jnp.int32, (half, half), 1)

    def pack():
        first = inverse[pl.ds(0, half), pl.ds(0, half)]
        second = inverse[pl.ds(half, half), pl.ds(half, half)]
        packed[pl.ds(0, half)] = jnp.where(block_row >= block_column, first, second.T)
        diagonal = jnp.where(block_row == block_column, second, 0.0)
        packed[pl.ds(half, 8)] = jnp.broadcast_to(
            jnp.sum(diagonal, axis=0, keepdims=True), (8, half)
        )

    def unpack():
        both = packed[pl.ds(0, half)]
        diagonal = packed[pl.ds(half, 1)]
        zero = jnp.zeros((half, half), jnp.float32)
        first = jnp.where(block_row >= block_column, both, 0.0)
        second = jnp.where(block_row < block_column, both, 0.0)
        second = jnp.where(block_row == block_column, diagonal, second).T
        upper = jnp.concatenate([first, zero], axis=1)
        lower = jnp.concatenate([top_corner[...], second], axis=1)
        return jnp.concatenate([upper, lower], axis=0)

    @pl.when(jnp.logical_and(is_top, even))
    def _():
        pl.semaphore_wait(barrier, greetings)
        give_copy[0].start()
        corner_copy.start()
        rhs_load.start()
        inverse_load.wait()
        pack()
        packed_copy.start()
        for copy in give_copy[1:]:
            copy.start()
        rhs_load.wait()
        make_part()
        pair_copy.start()
        pair_copy.wait_send()
        corner_copy.wait_send()
        packed_copy.wait_send()
        all_sent(top_rhs.at[pl.ds(0, chunks - 1)], next_send)
        pl.semaphore_signal(clear_sem, inc=1, device_id=right, device_id_type=MESH)
        give_copy[chunks - 1].wait_send()
        mate_copy.wait_recv()
        make_factor()
        for c in range(chunks):
            lift_copy[c].wait_recv()
            store(c, solved[c])

    @pl.when(jnp.logical_and(is_top, odd))
    def _():
        rhs_load.wait()
        make_part()
        inverse_load.wait()
        gram[...] = squared(inverse[...])
        pl.semaphore_wait(barrier, greetings)

        def solve(c):
            up_copy[c].wait_recv()
            solved[c] = product(gram[...], right_operand(rhs[:, spans[c]] - up_in[c]))
            if c == 0:
                pl.semaphore_wait(clear_sem, 1)
            if split and c == final:
                body_down.start()
                tail_across.start()
                tail_down.start()
            else:
                down_copy[c].start()

        pair_copy.wait_recv()
        rise_copy.wait_recv()
        gathered[...] = part[...] + pair_in[...] + rise_in[...]
        for copy in hub_copy:
            copy.start()
        for c in range(chunks - 1):
            solve(c)
        hubs_all.wait_recv()
        value = gathered[...]
        for j in range(hubs - 1):
            value = value + hub_in[j]
        total_in[...] = value
        fall_copy.start()
        mate_copy.start()
        solve(chunks - 1)
        make_factor()
        for c in range(chunks):
            store(c, solved[c])
        hubs_all.wait_send()
        fall_copy.wait_send()
        mate_copy.wait_send()
        if split:
            tail_across.wait_send()
        all_sent(solved, down_send)

    def make_spread():
        operand = right_operand(inverse[...])
        spread_next[...] = left_operand(product(block_next[...], operand))
        spread_own[...] = left_operand(product(block_own[...], operand))

    def make_turned():
        for matrix, turned in ((spread_own, turned_own), (spread_next, turned_next)):
            for piece in range(2):
                span = pl.ds(piece * width, width)
                turned[:, span] = matrix[:, span].T

    def take(c):
        value = rhs[:, spans[c]]
        if levels > 2:

            @pl.when(level > 0)
            def _():
                up_copy[c].wait_recv()

            value = value - jnp.where(level > 0, up_in[c], 0.0)
        operand = right_operand(value)
        operands[c] = operand
        forwards[c] = right_operand(product(inverse_left[...], operand))

    def make_base():
        gram[...] = squared(inverse[...])
        for c in range(chunks):
            base[c] = product(gram[...], operands[c])

    def send_next(c):
        take(c)
        if c == 0:
            rows_load.wait()
            block_load.wait()
            block_next[...] = picked(slots // 2)
        next_out[c] = product(block_next[...], forwards[c])
        if c == 0:
            pl.semaphore_wait(barrier, greetings)
        next_copy[c].start()
        if c == 0:
            rest_load.wait()
            make_part()

            @pl.when(even)
            def _():
                pair_copy.start()

    def start_up():
        inverse_load.wait()
        inverse_left[...] = left_operand(inverse[...])
        head_load.wait()

    def send_side(c):
        if c == 0 and detour:

            @pl.when(is_sender)
            def _():
                for copy in away_copy:
                    copy.start()

            @pl.when(jnp.logical_not(is_sender))
            def _():
                side_copy[c].start()

        else:
            side_copy[c].start()

    def pass_on():
        if detour:

            @pl.when(is_relay)
            def _():
                away_copy[0].wait_recv()

            for i, number in enumerate(RELAYS):

                @pl.when(jnp.logical_and(has_up, sub == number))
                def _():
                    relay_copy[i].start()

    def hand_down(c, value):
        if levels > 2:

            @pl.when(level > 0)
            def _():
                solved[c] = value
                down_copy[c].start()

    def await_down():
        if levels > 2:

            @pl.when(level > 0)
            def _():
                all_sent(solved, down_send)

    @pl.when(is_host)
    def _():
        start_up()
        for c in range(chunks):
            send_next(c)
        block_own[...] = picked(0)
        for c in range(chunks):
            own[c] = product(block_own[...], forwards[c])
        make_spread()
        make_turned()
        make_base()
        corner_copy.wait_recv()
        packed_copy.wait_recv()
        gram_top[...] = squared(unpack())
        for c in range(chunks):
            next_copy[c].wait_recv()
            give_copy[c].wait_recv()
            operand = right_operand(top_rhs[c] - (own[c] + next_in[c]))
            value = product(gram_top[...], operand)
            own_in[c] = value
            send_side(c)
            lift_copy[c].start()
            base[c] = base[c] - product(turned_own[...], right_operand(value))
        for c in range(chunks):
            if c == chunks - 1:
                mate_copy.wait_recv()
                make_factor()
                for d in range(c):
                    store(d, base[d])
            side_copy[c].wait_recv()
            value = base[c] - product(turned_next[...], right_operand(beside_in[c]))
            hand_down(c, value)
            if c == chunks - 1:
                store(c, value)
            else:
                base[c] = value
        pair_copy.wait_send()
        all_sent(next_out, next_send)
        all_sent(own_in, up_send)
        all_sent(own_in, side_send)
        await_down()

    def climb(leads):
        start_up()
        early = min(2, chunks)
        for c in range(early):
            send_next(c)
        block_own[...] = picked(0)
        for c in range(early):
            own[c] = product(block_own[...], forwards[c])
        if leads:
            gather_pair()
            rise_copy.start()
        for c in range(early):
            next_copy[c].wait_recv()
            own[c] = own[c] + next_in[c]
            up_copy[c].start()
        for c in range(early, chunks):
            send_next(c)
            own[c] = product(block_own[...], forwards[c])
        for c in range(early, chunks):
            next_copy[c].wait_recv()
            own[c] = own[c] + next_in[c]
            up_copy[c].start()
        make_spread()
        make_turned()
        make_base()
        if leads:
            pass_on()

        def spread_total():
            if leads:
                fall_copy.wait_recv()
                mate_copy.start()
                if levels > 2:

                    @pl.when(level > 0)
                    def _():
                        fall_copy.start()

                make_factor()

        def take_down(c):
            if split and leads and c == final:
                body_down.wait_recv()
                body_side.start()
            else:
                down_copy[c].wait_recv()
                send_side(c)

        def own_part(c):
            if split and leads and c == final:
                tail_down.wait_recv()
            base[c] = base[c] - product(turned_own[...], right_operand(own_in[c]))

        def beside_part(c, known):
            side_copy[c].wait_recv()
            value = base[c] - product(turned_next[...], right_operand(beside_in[c]))
            hand_down(c, value)
            if leads and known:
                store(c, value)
            else:
                base[c] = value

        for c in range(final):
            take_down(c)
            own_part(c)
            if c > 0:
                beside_part(c, False)
        spread_total()
        if leads:
            for c in range(1, final):
                store(c, base[c])
        take_down(final)
        own_part(final)
        if final > 0:
            beside_part(0, True)
        beside_part(final, True)
        if not leads:
            mate_copy.wait_recv()
            make_factor()
            for c in range(chunks):
                store(c, base[c])
        all_sent(next_out, next_send)
        all_sent(own, up_send)
        if split and leads:
            all_sent(own_in.at[:, pl.ds(0, width - TAIL_ROWS // chunks)], side_send)
        else:
            all_sent(own_in, side_send)
        if leads and detour:

            @pl.when(is_relay)
            def _():
                all_sent(relayed, sums_send.at[0])

        if leads:
            rise_copy.wait_send()
            mate_copy.wait_send()
            if levels > 2:

                @pl.when(level > 0)
                def _():
                    fall_copy.wait_send()
        else:
            pair_copy.wait_send()
        await_down()

    @pl.when(jnp.logical_and(has_up, odd))
    def _():
        climb(True)

    if levels > 2:

        @pl.when(jnp.logical_and(level < levels - 2, even))
        def _():
            climb(False)


def per_device(factor_inv, update_blocks, update_rows, right_side):
    levels = lax.axis_size("level")
    subs = lax.axis_size("sub")
    width = factor_inv.shape[-1]
    columns = right_side.shape[-1]
    slots, block_rows = update_blocks.shape[2:4]
    chunks = columns // LANES
    hubs = subs // 2
    piece = pltpu.VMEM((chunks, width, LANES), jnp.float32)
    wide = pltpu.VMEM((width, 2 * width), jnp.bfloat16)
    line = pltpu.VMEM((1, columns), jnp.float32)
    chunk_sem = pltpu.SemaphoreType.DMA((chunks,))
    in_hbm = pl.BlockSpec(memory_space=pltpu.HBM)
    held = [
        pltpu.with_memory_space_constraint(array, pltpu.HBM)
        for array in (update_rows[0, 0], factor_inv[0, 0], update_blocks[0, 0], right_side[0, 0])
    ]
    value = pl.pallas_call(
        functools.partial(kernel, levels, subs),
        out_shape=jax.ShapeDtypeStruct((width, columns), jnp.float32),
        in_specs=[in_hbm] * 4,
        out_specs=pl.BlockSpec(memory_space=pltpu.VMEM),
        scratch_shapes=[
            pltpu.SMEM((slots,), jnp.int32),
            pltpu.VMEM((width, width), jnp.float32),
            pltpu.VMEM((slots, block_rows, width), jnp.float32),
            pltpu.VMEM((width, columns), jnp.float32),
            pltpu.VMEM((chunks, width, 2 * LANES), jnp.bfloat16),
            pltpu.VMEM((chunks, width, 2 * LANES), jnp.bfloat16),
        ]
        + [wide] * 9
        + [piece] * 7
        + [pltpu.VMEM((width // len(RELAYS), LANES), jnp.float32), piece]
        + [
            pltpu.VMEM((width // 2 + 8, width // 2), jnp.float32),
            pltpu.VMEM((width // 2, width // 2), jnp.float32),
            piece,
        ]
        + [line] * 4
        + [pltpu.VMEM((hubs - 1, 1, columns), jnp.float32)]
        + [line] * 2
        + [pltpu.SemaphoreType.DMA]
        + [pltpu.SemaphoreType.DMA((chunks if levels == 2 else 2 * chunks,))]
        + [pltpu.SemaphoreType.DMA]
        + [pltpu.SemaphoreType.DMA, chunk_sem] * 2
        + [pltpu.SemaphoreType.DMA((4,)), pltpu.SemaphoreType.DMA((3,))]
        + [pltpu.SemaphoreType.REGULAR]
        + [pltpu.SemaphoreType.DMA],
        compiler_params=pltpu.CompilerParams(
            collective_id=0, has_side_effects=True, vmem_limit_bytes=32 * 1024 * 1024
        ),
        name="staircase",
    )(*held)
    return value[None, None]


def solution(mesh):
    return jax.shard_map(
        per_device,
        mesh=mesh,
        in_specs=(
            P("level", "sub", None, None),
            P("level", "sub", None, None, None),
            P("level", "sub", None),
            P("level", "sub", None, None),
        ),
        out_specs=P("level", "sub", None, None),
        check_vma=False,
    )
```

```python
import functools

import jax
import jax.numpy as jnp
from jax import lax
from jax.experimental import pallas as pl
from jax.experimental.pallas import tpu as pltpu
from jax.sharding import PartitionSpec as P

LANES = 128
SENDER, RELAYS, RECEIVER = 2, (5, 9), 1
TAIL_ROWS = 96
MESH = pl.DeviceIdType.MESH


def halves(value):
    high = value.astype(jnp.bfloat16)
    low = (value - high.astype(jnp.float32)).astype(jnp.bfloat16)
    return high, low


def left_operand(matrix):
    high, low = halves(matrix)
    return jnp.concatenate([high, low], axis=1)


def right_operand(values):
    high, low = halves(values)
    return jnp.concatenate([high, low], axis=1)


def product(left, right):
    depth, columns = right.shape[0], right.shape[1] // 2
    upper = jnp.dot(left[:, :depth], right, preferred_element_type=jnp.float32)
    lower = jnp.dot(left[:, depth:], right[:, :columns], preferred_element_type=jnp.float32)
    return upper[:, :columns] + (upper[:, columns:] + lower)


def kernel(
    levels,
    subs,
    rows_hbm,
    inverse_hbm,
    blocks_hbm,
    rhs_hbm,
    x_ref,
    rows,
    inverse,
    blocks,
    rhs,
    operands,
    forwards,
    inverse_left,
    block_own,
    block_next,
    spread_own,
    spread_next,
    turned_own,
    turned_next,
    gram,
    gram_top,
    base,
    own,
    next_out,
    next_in,
    up_in,
    own_in,
    beside_in,
    relayed,
    solved,
    packed,
    top_corner,
    top_rhs,
    part,
    pair_in,
    rise_in,
    gathered,
    hub_in,
    total_in,
    factor,
    next_send,
    next_recv,
    up_send,
    down_send,
    down_recv,
    side_send,
    side_recv,
    sums_send,
    sums_recv,
    clear_sem,
    relay_recv,
):
    level = lax.axis_index("level")
    sub = lax.axis_index("sub")
    chunks = rhs.shape[1] // LANES
    width = inverse.shape[0]
    half = width // 2
    slots = blocks.shape[0]
    hubs = subs // 2
    right = {"sub": lax.rem(sub + 1, subs)}
    left = {"sub": lax.rem(sub + subs - 1, subs)}
    detour = subs > max(RELAYS)
    share = width // len(RELAYS)
    above = {"level": level + 1}
    below = {"level": level - 1}
    others = [{"sub": lax.rem(sub + 2 * j, subs)} for j in range(1, hubs)]
    even = lax.rem(sub, 2) == 0
    odd = jnp.logical_not(even)
    is_top = level == levels - 1
    has_up = level < levels - 1
    is_host = jnp.logical_and(level == levels - 2, even)

    rows_load = pltpu.make_async_copy(rows_hbm, rows, down_send)
    block_load = pltpu.make_async_copy(blocks_hbm, blocks, up_send)
    inverse_load = pltpu.make_async_copy(inverse_hbm, inverse, sums_send.at[3])
    head, rest = pl.ds(0, LANES), pl.ds(LANES, rhs.shape[1] - LANES)
    head_load = pltpu.make_async_copy(rhs_hbm.at[:, head], rhs.at[:, head], sums_send.at[1])
    rest_load = pltpu.make_async_copy(rhs_hbm.at[:, rest], rhs.at[:, rest], sums_send.at[2])
    rhs_load = pltpu.make_async_copy(rhs_hbm, rhs, sums_send.at[2])
    spans = [pl.ds(c * LANES, LANES) for c in range(chunks)]

    barrier = pltpu.get_barrier_semaphore()

    def greet(device):
        pl.semaphore_signal(barrier, inc=1, device_id=device, device_id_type=MESH)

    @pl.when(has_up)
    def _():
        greet(left)
        greet(above)

    @pl.when(jnp.logical_and(has_up, even))
    def _():
        greet(right)

    is_sender = jnp.logical_and(has_up, sub == SENDER)
    is_relay = jnp.logical_and(has_up, sub == RELAYS[0])
    for number in RELAYS[1:]:
        is_relay = jnp.logical_or(is_relay, jnp.logical_and(has_up, sub == number))
    if detour:

        @pl.when(is_relay)
        def _():
            greet({"sub": SENDER})

        @pl.when(jnp.logical_and(has_up, sub == RECEIVER))
        def _():
            for number in RELAYS:
                greet({"sub": number})

    @pl.when(level > 0)
    def _():
        greet(below)

    @pl.when(jnp.logical_and(is_top, even))
    def _():
        greet(right)

    @pl.when(jnp.logical_and(is_top, odd))
    def _():
        greet(left)
        for device in others:
            greet(device)

    greetings = jnp.where(even, 1, jnp.where(is_top, hubs, 2)) + jnp.where(has_up, 1, 0)
    greetings += jnp.where(level > 0, 1, 0)
    if detour:
        greetings += jnp.where(is_sender, len(RELAYS), jnp.where(is_relay, 1, 0))

    inverse_load.start()

    @pl.when(jnp.logical_and(is_top, odd))
    def _():
        rhs_load.start()

    @pl.when(has_up)
    def _():
        head_load.start()
        rows_load.start()
        block_load.start()
        rest_load.start()

    def remote(source, target, send, recv, device):
        return pltpu.make_async_remote_copy(
            src_ref=source,
            dst_ref=target,
            send_sem=send,
            recv_sem=recv,
            device_id=device,
            device_id_type=MESH,
        )

    def chunk_copies(source, target, send, recv, device, base=0):
        return [
            remote(source.at[c], target.at[c], send, recv.at[base + c], device)
            for c in range(chunks)
        ]

    def all_sent(array, send):
        remote(array, array, send, send, left).wait_send()

    corner_copy = remote(
        inverse_hbm.at[pl.ds(half, half), pl.ds(0, half)],
        top_corner,
        up_send,
        sums_recv.at[0],
        below,
    )
    packed_copy = remote(packed, packed, down_send, sums_recv.at[1], below)
    give_copy = [
        remote(
            rhs_hbm.at[:, spans[c]],
            top_rhs.at[c],
            next_send if c < chunks - 1 else side_send,
            down_recv.at[c],
            below,
        )
        for c in range(chunks)
    ]
    next_copy = chunk_copies(next_out, next_in, next_send, next_recv, right)
    arrival = 0 if levels == 2 else chunks
    up_copy = chunk_copies(own, up_in, up_send, next_recv, above, arrival)
    lift_copy = chunk_copies(own_in, solved, up_send, next_recv, above, arrival)
    down_copy = chunk_copies(solved, own_in, down_send, down_recv, below)
    side_copy = chunk_copies(own_in, beside_in, side_send, side_recv, left)
    away_copy = [
        remote(
            own_in.at[0, pl.ds(i * share, share)],
            relayed,
            side_send,
            relay_recv,
            {"sub": RELAYS[i]},
        )
        for i in range(len(RELAYS))
    ]
    relay_copy = [
        remote(
            relayed,
            beside_in.at[0, pl.ds(i * share, share)],
            sums_send.at[0],
            side_recv.at[0],
            {"sub": RECEIVER},
        )
        for i in range(len(RELAYS))
    ]
    split = levels == 2 and chunks > 1 and TAIL_ROWS % chunks == 0
    final = chunks - 1
    body = width - TAIL_ROWS
    body_rows, tail_rows = pl.ds(0, body), pl.ds(body, TAIL_ROWS)
    body_down = remote(
        solved.at[final, body_rows],
        own_in.at[final, body_rows],
        down_send,
        down_recv.at[final],
        below,
    )
    tail_down = remote(
        solved.at[final, tail_rows],
        own_in.at[final, tail_rows],
        down_send,
        sums_recv.at[1],
        below,
    )
    tail_across = remote(
        solved.at[final, tail_rows],
        beside_in.at[final, tail_rows],
        sums_send.at[0],
        side_recv.at[final],
        {"level": level - 1, "sub": lax.rem(sub + subs - 1, subs)},
    )
    body_side = remote(
        own_in.at[final, body_rows],
        beside_in.at[final, body_rows],
        side_send,
        side_recv.at[final],
        left,
    )
    pair_copy = remote(part, pair_in, sums_send.at[0], sums_recv.at[0], right)
    rise_copy = remote(gathered, rise_in, sums_send.at[1], sums_recv.at[1], above)
    fall_copy = remote(total_in, total_in, sums_send.at[2], sums_recv.at[2], below)
    mate_copy = remote(total_in, total_in, sums_send.at[3], sums_recv.at[2], left)
    hub_copy = [
        remote(gathered, hub_in.at[j], side_send, side_recv.at[0], others[j])
        for j in range(hubs - 1)
    ]
    hubs_all = remote(hub_in, hub_in, side_send, side_recv.at[0], left)

    def placed(slot):
        found = jnp.int32(0)
        for k in range(slots):
            found = jnp.where(rows[k] == slot, k, found)
        return blocks[found]

    def picked(first):
        return left_operand(
            jnp.concatenate([placed(first + d) for d in range(slots // 2)], axis=0)
        )

    def squared(matrix):
        return left_operand(product(left_operand(matrix.T), right_operand(matrix)))

    def make_part():
        for span in spans:
            value = rhs[:, span]
            part[:, span] = jnp.sum(value * value, axis=0, keepdims=True)

    def gather_pair():
        pair_copy.wait_recv()
        if levels > 2:

            @pl.when(level > 0)
            def _():
                rise_copy.wait_recv()

            gathered[...] = part[...] + pair_in[...] + jnp.where(level > 0, rise_in[...], 0.0)
        else:
            gathered[...] = part[...] + pair_in[...]

    def make_factor():
        factor[...] = 1.0 / jnp.sqrt(total_in[...] / (levels * subs * width) + 1e-06)

    def store(c, value):
        x_ref[:, spans[c]] = value * factor[:, spans[c]]

    block_row = lax.broadcasted_iota(jnp.int32, (half, half), 0)
    block_column = lax.broadcasted_iota(jnp.int32, (half, half), 1)

    def pack():
        first = inverse[pl.ds(0, half), pl.ds(0, half)]
        second = inverse[pl.ds(half, half), pl.ds(half, half)]
        packed[pl.ds(0, half)] = jnp.where(block_row >= block_column, first, second.T)
        diagonal = jnp.where(block_row == block_column, second, 0.0)
        packed[pl.ds(half, 8)] = jnp.broadcast_to(
            jnp.sum(diagonal, axis=0, keepdims=True), (8, half)
        )

    def unpack():
        both = packed[pl.ds(0, half)]
        diagonal = packed[pl.ds(half, 1)]
        zero = jnp.zeros((half, half), jnp.float32)
        first = jnp.where(block_row >= block_column, both, 0.0)
        second = jnp.where(block_row < block_column, both, 0.0)
        second = jnp.where(block_row == block_column, diagonal, second).T
        upper = jnp.concatenate([first, zero], axis=1)
        lower = jnp.concatenate([top_corner[...], second], axis=1)
        return jnp.concatenate([upper, lower], axis=0)

    @pl.when(jnp.logical_and(is_top, even))
    def _():
        pl.semaphore_wait(barrier, greetings)
        give_copy[0].start()
        corner_copy.start()
        rhs_load.start()
        inverse_load.wait()
        pack()
        packed_copy.start()
        for copy in give_copy[1:]:
            copy.start()
        rhs_load.wait()
        make_part()
        pair_copy.start()
        pair_copy.wait_send()
        corner_copy.wait_send()
        packed_copy.wait_send()
        all_sent(top_rhs.at[pl.ds(0, chunks - 1)], next_send)
        pl.semaphore_signal(clear_sem, inc=1, device_id=right, device_id_type=MESH)
        give_copy[chunks - 1].wait_send()
        mate_copy.wait_recv()
        make_factor()
        for c in range(chunks):
            lift_copy[c].wait_recv()
            store(c, solved[c])

    @pl.when(jnp.logical_and(is_top, odd))
    def _():
        rhs_load.wait()
        make_part()
        inverse_load.wait()
        gram[...] = squared(inverse[...])
        pl.semaphore_wait(barrier, greetings)

        def solve(c):
            up_copy[c].wait_recv()
            solved[c] = product(gram[...], right_operand(rhs[:, spans[c]] - up_in[c]))
            if c == 0:
                pl.semaphore_wait(clear_sem, 1)
            if split and c == final:
                body_down.start()
                tail_across.start()
                tail_down.start()
            else:
                down_copy[c].start()

        pair_copy.wait_recv()
        rise_copy.wait_recv()
        gathered[...] = part[...] + pair_in[...] + rise_in[...]
        for copy in hub_copy:
            copy.start()
        for c in range(chunks - 1):
            solve(c)
        hubs_all.wait_recv()
        value = gathered[...]
        for j in range(hubs - 1):
            value = value + hub_in[j]
        total_in[...] = value
        fall_copy.start()
        mate_copy.start()
        solve(chunks - 1)
        make_factor()
        for c in range(chunks):
            store(c, solved[c])
        hubs_all.wait_send()
        fall_copy.wait_send()
        mate_copy.wait_send()
        if split:
            tail_across.wait_send()
        all_sent(solved, down_send)

    def make_spread():
        operand = right_operand(inverse[...])
        spread_next[...] = left_operand(product(block_next[...], operand))
        spread_own[...] = left_operand(product(block_own[...], operand))

    def make_turned():
        for matrix, turned in ((spread_own, turned_own), (spread_next, turned_next)):
            for piece in range(2):
                span = pl.ds(piece * width, width)
                turned[:, span] = matrix[:, span].T

    def take(c):
        value = rhs[:, spans[c]]
        if levels > 2:

            @pl.when(level > 0)
            def _():
                up_copy[c].wait_recv()

            value = value - jnp.where(level > 0, up_in[c], 0.0)
        operand = right_operand(value)
        operands[c] = operand
        forwards[c] = right_operand(product(inverse_left[...], operand))

    def make_base():
        gram[...] = squared(inverse[...])
        for c in range(chunks):
            base[c] = product(gram[...], operands[c])

    def send_next(c):
        take(c)
        if c == 0:
            rows_load.wait()
            block_load.wait()
            block_next[...] = picked(slots // 2)
        next_out[c] = product(block_next[...], forwards[c])
        if c == 0:
            pl.semaphore_wait(barrier, greetings)
        next_copy[c].start()
        if c == 0:
            rest_load.wait()
            make_part()

            @pl.when(even)
            def _():
                pair_copy.start()

    def start_up():
        inverse_load.wait()
        inverse_left[...] = left_operand(inverse[...])
        head_load.wait()

    def send_side(c):
        if c == 0 and detour:

            @pl.when(is_sender)
            def _():
                for copy in away_copy:
                    copy.start()

            @pl.when(jnp.logical_not(is_sender))
            def _():
                side_copy[c].start()

        else:
            side_copy[c].start()

    def pass_on():
        if detour:

            @pl.when(is_relay)
            def _():
                away_copy[0].wait_recv()

            for i, number in enumerate(RELAYS):

                @pl.when(jnp.logical_and(has_up, sub == number))
                def _():
                    relay_copy[i].start()

    def hand_down(c, value):
        if levels > 2:

            @pl.when(level > 0)
            def _():
                solved[c] = value
                down_copy[c].start()

    def await_down():
        if levels > 2:

            @pl.when(level > 0)
            def _():
                all_sent(solved, down_send)

    @pl.when(is_host)
    def _():
        start_up()
        for c in range(chunks):
            send_next(c)
        block_own[...] = picked(0)
        for c in range(chunks):
            own[c] = product(block_own[...], forwards[c])
        make_spread()
        make_turned()
        make_base()
        corner_copy.wait_recv()
        packed_copy.wait_recv()
        gram_top[...] = squared(unpack())
        for c in range(chunks):
            next_copy[c].wait_recv()
            give_copy[c].wait_recv()
            operand = right_operand(top_rhs[c] - (own[c] + next_in[c]))
            value = product(gram_top[...], operand)
            own_in[c] = value
            send_side(c)
            lift_copy[c].start()
            base[c] = base[c] - product(turned_own[...], right_operand(value))
        for c in range(chunks):
            if c == chunks - 1:
                mate_copy.wait_recv()
                make_factor()
                for d in range(c):
                    store(d, base[d])
            side_copy[c].wait_recv()
            value = base[c] - product(turned_next[...], right_operand(beside_in[c]))
            hand_down(c, value)
            if c == chunks - 1:
                store(c, value)
            else:
                base[c] = value
        pair_copy.wait_send()
        all_sent(next_out, next_send)
        all_sent(own_in, up_send)
        all_sent(own_in, side_send)
        await_down()

    def climb(leads):
        start_up()
        early = min(2, chunks)
        for c in range(early):
            send_next(c)
        block_own[...] = picked(0)
        for c in range(early):
            own[c] = product(block_own[...], forwards[c])
        if leads:
            gather_pair()
            rise_copy.start()
        for c in range(early):
            next_copy[c].wait_recv()
            own[c] = own[c] + next_in[c]
            up_copy[c].start()
        for c in range(early, chunks):
            send_next(c)
            own[c] = product(block_own[...], forwards[c])
        for c in range(early, chunks):
            next_copy[c].wait_recv()
            own[c] = own[c] + next_in[c]
            up_copy[c].start()
        make_spread()
        make_turned()
        make_base()
        if leads:
            pass_on()

        def spread_total():
            if leads:
                fall_copy.wait_recv()
                mate_copy.start()
                if levels > 2:

                    @pl.when(level > 0)
                    def _():
                        fall_copy.start()

                make_factor()

        def take_down(c):
            if split and leads and c == final:
                body_down.wait_recv()
                body_side.start()
            else:
                down_copy[c].wait_recv()
                send_side(c)

        def own_part(c):
            if split and leads and c == final:
                tail_down.wait_recv()
            base[c] = base[c] - product(turned_own[...], right_operand(own_in[c]))

        def beside_part(c, known):
            side_copy[c].wait_recv()
            value = base[c] - product(turned_next[...], right_operand(beside_in[c]))
            hand_down(c, value)
            if leads and known:
                store(c, value)
            else:
                base[c] = value

        for c in range(final):
            take_down(c)
            own_part(c)
            if c > 0:
                beside_part(c, False)
        spread_total()
        if leads:
            for c in range(1, final):
                store(c, base[c])
        take_down(final)
        if split and leads:
            tail_down.wait_recv()
            side_copy[0].wait_recv()
            own_last = product(turned_own[...], right_operand(own_in[final]))
            beside_first = product(turned_next[...], right_operand(beside_in[0]))
            base[final] = base[final] - own_last
            store(0, base[0] - beside_first)
        else:
            own_part(final)
            if final > 0:
                beside_part(0, True)
        beside_part(final, True)
        if not leads:
            mate_copy.wait_recv()
            make_factor()
            for c in range(chunks):
                store(c, base[c])
        all_sent(next_out, next_send)
        all_sent(own, up_send)
        if split and leads:
            all_sent(own_in.at[:, pl.ds(0, width - TAIL_ROWS // chunks)], side_send)
        else:
            all_sent(own_in, side_send)
        if leads and detour:

            @pl.when(is_relay)
            def _():
                all_sent(relayed, sums_send.at[0])

        if leads:
            rise_copy.wait_send()
            mate_copy.wait_send()
            if levels > 2:

                @pl.when(level > 0)
                def _():
                    fall_copy.wait_send()
        else:
            pair_copy.wait_send()
        await_down()

    @pl.when(jnp.logical_and(has_up, odd))
    def _():
        climb(True)

    if levels > 2:

        @pl.when(jnp.logical_and(level < levels - 2, even))
        def _():
            climb(False)


def per_device(factor_inv, update_blocks, update_rows, right_side):
    levels = lax.axis_size("level")
    subs = lax.axis_size("sub")
    width = factor_inv.shape[-1]
    columns = right_side.shape[-1]
    slots, block_rows = update_blocks.shape[2:4]
    chunks = columns // LANES
    hubs = subs // 2
    piece = pltpu.VMEM((chunks, width, LANES), jnp.float32)
    wide = pltpu.VMEM((width, 2 * width), jnp.bfloat16)
    line = pltpu.VMEM((1, columns), jnp.float32)
    chunk_sem = pltpu.SemaphoreType.DMA((chunks,))
    in_hbm = pl.BlockSpec(memory_space=pltpu.HBM)
    held = [
        pltpu.with_memory_space_constraint(array, pltpu.HBM)
        for array in (update_rows[0, 0], factor_inv[0, 0], update_blocks[0, 0], right_side[0, 0])
    ]
    value = pl.pallas_call(
        functools.partial(kernel, levels, subs),
        out_shape=jax.ShapeDtypeStruct((width, columns), jnp.float32),
        in_specs=[in_hbm] * 4,
        out_specs=pl.BlockSpec(memory_space=pltpu.VMEM),
        scratch_shapes=[
            pltpu.SMEM((slots,), jnp.int32),
            pltpu.VMEM((width, width), jnp.float32),
            pltpu.VMEM((slots, block_rows, width), jnp.float32),
            pltpu.VMEM((width, columns), jnp.float32),
            pltpu.VMEM((chunks, width, 2 * LANES), jnp.bfloat16),
            pltpu.VMEM((chunks, width, 2 * LANES), jnp.bfloat16),
        ]
        + [wide] * 9
        + [piece] * 7
        + [pltpu.VMEM((width // len(RELAYS), LANES), jnp.float32), piece]
        + [
            pltpu.VMEM((width // 2 + 8, width // 2), jnp.float32),
            pltpu.VMEM((width // 2, width // 2), jnp.float32),
            piece,
        ]
        + [line] * 4
        + [pltpu.VMEM((hubs - 1, 1, columns), jnp.float32)]
        + [line] * 2
        + [pltpu.SemaphoreType.DMA]
        + [pltpu.SemaphoreType.DMA((chunks if levels == 2 else 2 * chunks,))]
        + [pltpu.SemaphoreType.DMA]
        + [pltpu.SemaphoreType.DMA, chunk_sem] * 2
        + [pltpu.SemaphoreType.DMA((4,)), pltpu.SemaphoreType.DMA((3,))]
        + [pltpu.SemaphoreType.REGULAR]
        + [pltpu.SemaphoreType.DMA],
        compiler_params=pltpu.CompilerParams(
            collective_id=0, has_side_effects=True, vmem_limit_bytes=32 * 1024 * 1024
        ),
        name="staircase",
    )(*held)
    return value[None, None]


def solution(mesh):
    return jax.shard_map(
        per_device,
        mesh=mesh,
        in_specs=(
            P("level", "sub", None, None),
            P("level", "sub", None, None, None),
            P("level", "sub", None),
            P("level", "sub", None, None),
        ),
        out_specs=P("level", "sub", None, None),
        check_vma=False,
    )
```

```python
import functools

import jax
import jax.numpy as jnp
from jax import lax
from jax.experimental import pallas as pl
from jax.experimental.pallas import tpu as pltpu
from jax.sharding import PartitionSpec as P

LANES = 128
SENDER, RELAYS, RECEIVER = 2, (5, 9), 1
TAIL_ROWS = 96
MESH = pl.DeviceIdType.MESH


def halves(value):
    high = value.astype(jnp.bfloat16)
    low = (value - high.astype(jnp.float32)).astype(jnp.bfloat16)
    return high, low


def left_operand(matrix):
    high, low = halves(matrix)
    return jnp.concatenate([high, low], axis=1)


def right_operand(values):
    high, low = halves(values)
    return jnp.concatenate([high, low], axis=1)


def product(left, right):
    depth, columns = right.shape[0], right.shape[1] // 2
    upper = jnp.dot(left[:, :depth], right, preferred_element_type=jnp.float32)
    lower = jnp.dot(left[:, depth:], right[:, :columns], preferred_element_type=jnp.float32)
    return upper[:, :columns] + (upper[:, columns:] + lower)


def kernel(
    levels,
    subs,
    rows_hbm,
    inverse_hbm,
    blocks_hbm,
    rhs_hbm,
    x_ref,
    rows,
    inverse,
    blocks,
    rhs,
    operands,
    forwards,
    inverse_left,
    block_own,
    block_next,
    spread_own,
    spread_next,
    turned_own,
    turned_next,
    gram,
    gram_top,
    base,
    own,
    next_out,
    next_in,
    up_in,
    own_in,
    beside_in,
    relayed,
    solved,
    packed,
    top_corner,
    top_rhs,
    part,
    pair_in,
    rise_in,
    gathered,
    hub_in,
    total_in,
    factor,
    next_send,
    next_recv,
    up_send,
    down_send,
    down_recv,
    side_send,
    side_recv,
    sums_send,
    sums_recv,
    clear_sem,
    relay_recv,
):
    level = lax.axis_index("level")
    sub = lax.axis_index("sub")
    chunks = rhs.shape[1] // LANES
    width = inverse.shape[0]
    half = width // 2
    slots = blocks.shape[0]
    hubs = subs // 2
    right = {"sub": lax.rem(sub + 1, subs)}
    left = {"sub": lax.rem(sub + subs - 1, subs)}
    detour = subs > max(RELAYS)
    share = width // len(RELAYS)
    above = {"level": level + 1}
    below = {"level": level - 1}
    others = [{"sub": lax.rem(sub + 2 * j, subs)} for j in range(1, hubs)]
    even = lax.rem(sub, 2) == 0
    odd = jnp.logical_not(even)
    is_top = level == levels - 1
    has_up = level < levels - 1
    is_host = jnp.logical_and(level == levels - 2, even)

    rows_load = pltpu.make_async_copy(rows_hbm, rows, down_send)
    block_load = pltpu.make_async_copy(blocks_hbm, blocks, up_send)
    inverse_load = pltpu.make_async_copy(inverse_hbm, inverse, sums_send.at[3])
    head, rest = pl.ds(0, LANES), pl.ds(LANES, rhs.shape[1] - LANES)
    head_load = pltpu.make_async_copy(rhs_hbm.at[:, head], rhs.at[:, head], sums_send.at[1])
    rest_load = pltpu.make_async_copy(rhs_hbm.at[:, rest], rhs.at[:, rest], sums_send.at[2])
    rhs_load = pltpu.make_async_copy(rhs_hbm, rhs, sums_send.at[2])
    spans = [pl.ds(c * LANES, LANES) for c in range(chunks)]

    barrier = pltpu.get_barrier_semaphore()

    def greet(device):
        pl.semaphore_signal(barrier, inc=1, device_id=device, device_id_type=MESH)

    @pl.when(has_up)
    def _():
        greet(left)
        greet(above)

    @pl.when(jnp.logical_and(has_up, even))
    def _():
        greet(right)

    is_sender = jnp.logical_and(has_up, sub == SENDER)
    is_relay = jnp.logical_and(has_up, sub == RELAYS[0])
    for number in RELAYS[1:]:
        is_relay = jnp.logical_or(is_relay, jnp.logical_and(has_up, sub == number))
    if detour:

        @pl.when(is_relay)
        def _():
            greet({"sub": SENDER})

        @pl.when(jnp.logical_and(has_up, sub == RECEIVER))
        def _():
            for number in RELAYS:
                greet({"sub": number})

    @pl.when(level > 0)
    def _():
        greet(below)

    @pl.when(jnp.logical_and(is_top, even))
    def _():
        greet(right)

    @pl.when(jnp.logical_and(is_top, odd))
    def _():
        greet(left)
        for device in others:
            greet(device)

    greetings = jnp.where(even, 1, jnp.where(is_top, hubs, 2)) + jnp.where(has_up, 1, 0)
    greetings += jnp.where(level > 0, 1, 0)
    if detour:
        greetings += jnp.where(is_sender, len(RELAYS), jnp.where(is_relay, 1, 0))

    inverse_load.start()

    @pl.when(jnp.logical_and(is_top, odd))
    def _():
        rhs_load.start()

    @pl.when(has_up)
    def _():
        head_load.start()
        rows_load.start()
        block_load.start()
        rest_load.start()

    def remote(source, target, send, recv, device):
        return pltpu.make_async_remote_copy(
            src_ref=source,
            dst_ref=target,
            send_sem=send,
            recv_sem=recv,
            device_id=device,
            device_id_type=MESH,
        )

    def chunk_copies(source, target, send, recv, device, base=0):
        return [
            remote(source.at[c], target.at[c], send, recv.at[base + c], device)
            for c in range(chunks)
        ]

    def all_sent(array, send):
        remote(array, array, send, send, left).wait_send()

    corner_copy = remote(
        inverse_hbm.at[pl.ds(half, half), pl.ds(0, half)],
        top_corner,
        up_send,
        sums_recv.at[0],
        below,
    )
    packed_copy = remote(packed, packed, down_send, sums_recv.at[1], below)
    give_copy = [
        remote(
            rhs_hbm.at[:, spans[c]],
            top_rhs.at[c],
            next_send if c < chunks - 1 else side_send,
            down_recv.at[c],
            below,
        )
        for c in range(chunks)
    ]
    next_copy = chunk_copies(next_out, next_in, next_send, next_recv, right)
    arrival = 0 if levels == 2 else chunks
    up_copy = chunk_copies(own, up_in, up_send, next_recv, above, arrival)
    lift_copy = chunk_copies(own_in, solved, up_send, next_recv, above, arrival)
    down_copy = chunk_copies(solved, own_in, down_send, down_recv, below)
    side_copy = chunk_copies(own_in, beside_in, side_send, side_recv, left)
    away_copy = [
        remote(
            own_in.at[0, pl.ds(i * share, share)],
            relayed,
            side_send,
            relay_recv,
            {"sub": RELAYS[i]},
        )
        for i in range(len(RELAYS))
    ]
    relay_copy = [
        remote(
            relayed,
            beside_in.at[0, pl.ds(i * share, share)],
            sums_send.at[0],
            side_recv.at[0],
            {"sub": RECEIVER},
        )
        for i in range(len(RELAYS))
    ]
    split = levels == 2 and chunks > 1 and TAIL_ROWS % chunks == 0
    final = chunks - 1
    body = width - TAIL_ROWS
    body_rows, tail_rows = pl.ds(0, body), pl.ds(body, TAIL_ROWS)
    body_down = remote(
        solved.at[final, body_rows],
        own_in.at[final, body_rows],
        down_send,
        down_recv.at[final],
        below,
    )
    tail_down = remote(
        solved.at[final, tail_rows],
        own_in.at[final, tail_rows],
        down_send,
        sums_recv.at[1],
        below,
    )
    tail_across = remote(
        solved.at[final, tail_rows],
        beside_in.at[final, tail_rows],
        sums_send.at[0],
        side_recv.at[final],
        {"level": level - 1, "sub": lax.rem(sub + subs - 1, subs)},
    )
    body_side = remote(
        own_in.at[final, body_rows],
        beside_in.at[final, body_rows],
        side_send,
        side_recv.at[final],
        left,
    )
    pair_copy = remote(part, pair_in, sums_send.at[0], sums_recv.at[0], right)
    rise_copy = remote(gathered, rise_in, sums_send.at[1], sums_recv.at[1], above)
    fall_copy = remote(total_in, total_in, sums_send.at[2], sums_recv.at[2], below)
    mate_copy = remote(total_in, total_in, sums_send.at[3], sums_recv.at[2], left)
    hub_copy = [
        remote(gathered, hub_in.at[j], side_send, side_recv.at[0], others[j])
        for j in range(hubs - 1)
    ]
    hubs_all = remote(hub_in, hub_in, side_send, side_recv.at[0], left)

    def placed(slot):
        found = jnp.int32(0)
        for k in range(slots):
            found = jnp.where(rows[k] == slot, k, found)
        return blocks[found]

    def picked(first):
        return left_operand(
            jnp.concatenate([placed(first + d) for d in range(slots // 2)], axis=0)
        )

    def squared(matrix):
        return left_operand(product(left_operand(matrix.T), right_operand(matrix)))

    def make_part():
        for span in spans:
            value = rhs[:, span]
            part[:, span] = jnp.sum(value * value, axis=0, keepdims=True)

    def gather_pair():
        pair_copy.wait_recv()
        if levels > 2:

            @pl.when(level > 0)
            def _():
                rise_copy.wait_recv()

            gathered[...] = part[...] + pair_in[...] + jnp.where(level > 0, rise_in[...], 0.0)
        else:
            gathered[...] = part[...] + pair_in[...]

    def make_factor():
        factor[...] = 1.0 / jnp.sqrt(total_in[...] / (levels * subs * width) + 1e-06)

    def store(c, value):
        x_ref[:, spans[c]] = value * factor[:, spans[c]]

    block_row = lax.broadcasted_iota(jnp.int32, (half, half), 0)
    block_column = lax.broadcasted_iota(jnp.int32, (half, half), 1)

    def pack():
        first = inverse[pl.ds(0, half), pl.ds(0, half)]
        second = inverse[pl.ds(half, half), pl.ds(half, half)]
        packed[pl.ds(0, half)] = jnp.where(block_row >= block_column, first, second.T)
        diagonal = jnp.where(block_row == block_column, second, 0.0)
        packed[pl.ds(half, 8)] = jnp.broadcast_to(
            jnp.sum(diagonal, axis=0, keepdims=True), (8, half)
        )

    def unpack():
        both = packed[pl.ds(0, half)]
        diagonal = packed[pl.ds(half, 1)]
        zero = jnp.zeros((half, half), jnp.float32)
        first = jnp.where(block_row >= block_column, both, 0.0)
        second = jnp.where(block_row < block_column, both, 0.0)
        second = jnp.where(block_row == block_column, diagonal, second).T
        upper = jnp.concatenate([first, zero], axis=1)
        lower = jnp.concatenate([top_corner[...], second], axis=1)
        return jnp.concatenate([upper, lower], axis=0)

    @pl.when(jnp.logical_and(is_top, even))
    def _():
        pl.semaphore_wait(barrier, greetings)
        give_copy[0].start()
        corner_copy.start()
        inverse_load.wait()
        pack()
        packed_copy.start()
        rhs_load.start()
        for copy in give_copy[1:]:
            copy.start()
        rhs_load.wait()
        make_part()
        pair_copy.start()
        pair_copy.wait_send()
        corner_copy.wait_send()
        packed_copy.wait_send()
        all_sent(top_rhs.at[pl.ds(0, chunks - 1)], next_send)
        pl.semaphore_signal(clear_sem, inc=1, device_id=right, device_id_type=MESH)
        give_copy[chunks - 1].wait_send()
        mate_copy.wait_recv()
        make_factor()
        for c in range(chunks):
            lift_copy[c].wait_recv()
            store(c, solved[c])

    @pl.when(jnp.logical_and(is_top, odd))
    def _():
        rhs_load.wait()
        make_part()
        inverse_load.wait()
        gram[...] = squared(inverse[...])
        pl.semaphore_wait(barrier, greetings)

        def solve(c):
            up_copy[c].wait_recv()
            solved[c] = product(gram[...], right_operand(rhs[:, spans[c]] - up_in[c]))
            if c == 0:
                pl.semaphore_wait(clear_sem, 1)
            if split and c == final:
                body_down.start()
                tail_across.start()
                tail_down.start()
            else:
                down_copy[c].start()

        pair_copy.wait_recv()
        rise_copy.wait_recv()
        gathered[...] = part[...] + pair_in[...] + rise_in[...]
        for copy in hub_copy:
            copy.start()
        for c in range(chunks - 1):
            solve(c)
        hubs_all.wait_recv()
        value = gathered[...]
        for j in range(hubs - 1):
            value = value + hub_in[j]
        total_in[...] = value
        fall_copy.start()
        mate_copy.start()
        solve(chunks - 1)
        make_factor()
        for c in range(chunks):
            store(c, solved[c])
        hubs_all.wait_send()
        fall_copy.wait_send()
        mate_copy.wait_send()
        if split:
            tail_across.wait_send()
        all_sent(solved, down_send)

    def make_spread():
        operand = right_operand(inverse[...])
        spread_next[...] = left_operand(product(block_next[...], operand))
        spread_own[...] = left_operand(product(block_own[...], operand))

    def make_turned():
        for matrix, turned in ((spread_own, turned_own), (spread_next, turned_next)):
            for piece in range(2):
                span = pl.ds(piece * width, width)
                turned[:, span] = matrix[:, span].T

    def take(c):
        value = rhs[:, spans[c]]
        if levels > 2:

            @pl.when(level > 0)
            def _():
                up_copy[c].wait_recv()

            value = value - jnp.where(level > 0, up_in[c], 0.0)
        operand = right_operand(value)
        operands[c] = operand
        forwards[c] = right_operand(product(inverse_left[...], operand))

    def make_base():
        gram[...] = squared(inverse[...])
        for c in range(chunks):
            base[c] = product(gram[...], operands[c])

    def send_next(c):
        take(c)
        if c == 0:
            rows_load.wait()
            block_load.wait()
            block_next[...] = picked(slots // 2)
        next_out[c] = product(block_next[...], forwards[c])
        if c == 0:
            pl.semaphore_wait(barrier, greetings)
        next_copy[c].start()
        if c == 0:
            rest_load.wait()
            make_part()

            @pl.when(even)
            def _():
                pair_copy.start()

    def start_up():
        inverse_load.wait()
        inverse_left[...] = left_operand(inverse[...])
        head_load.wait()

    def send_side(c):
        if c == 0 and detour:

            @pl.when(is_sender)
            def _():
                for copy in away_copy:
                    copy.start()

            @pl.when(jnp.logical_not(is_sender))
            def _():
                side_copy[c].start()

        else:
            side_copy[c].start()

    def pass_on():
        if detour:

            @pl.when(is_relay)
            def _():
                away_copy[0].wait_recv()

            for i, number in enumerate(RELAYS):

                @pl.when(jnp.logical_and(has_up, sub == number))
                def _():
                    relay_copy[i].start()

    def hand_down(c, value):
        if levels > 2:

            @pl.when(level > 0)
            def _():
                solved[c] = value
                down_copy[c].start()

    def await_down():
        if levels > 2:

            @pl.when(level > 0)
            def _():
                all_sent(solved, down_send)

    @pl.when(is_host)
    def _():
        start_up()
        for c in range(chunks):
            send_next(c)
        block_own[...] = picked(0)
        for c in range(chunks):
            own[c] = product(block_own[...], forwards[c])
        make_spread()
        make_turned()
        make_base()
        corner_copy.wait_recv()
        packed_copy.wait_recv()
        gram_top[...] = squared(unpack())
        for c in range(chunks):
            next_copy[c].wait_recv()
            give_copy[c].wait_recv()
            operand = right_operand(top_rhs[c] - (own[c] + next_in[c]))
            value = product(gram_top[...], operand)
            own_in[c] = value
            send_side(c)
            lift_copy[c].start()
            base[c] = base[c] - product(turned_own[...], right_operand(value))
        for c in range(chunks):
            if c == chunks - 1:
                mate_copy.wait_recv()
                make_factor()
                for d in range(c):
                    store(d, base[d])
            side_copy[c].wait_recv()
            value = base[c] - product(turned_next[...], right_operand(beside_in[c]))
            hand_down(c, value)
            if c == chunks - 1:
                store(c, value)
            else:
                base[c] = value
        pair_copy.wait_send()
        all_sent(next_out, next_send)
        all_sent(own_in, up_send)
        all_sent(own_in, side_send)
        await_down()

    def climb(leads):
        start_up()
        early = min(2, chunks)
        for c in range(early):
            send_next(c)
        block_own[...] = picked(0)
        for c in range(early):
            own[c] = product(block_own[...], forwards[c])
        if leads:
            gather_pair()
            rise_copy.start()
        for c in range(early):
            next_copy[c].wait_recv()
            own[c] = own[c] + next_in[c]
            up_copy[c].start()
        for c in range(early, chunks):
            send_next(c)
            own[c] = product(block_own[...], forwards[c])
        for c in range(early, chunks):
            next_copy[c].wait_recv()
            own[c] = own[c] + next_in[c]
            up_copy[c].start()
        make_spread()
        make_turned()
        make_base()
        if leads:
            pass_on()

        def spread_total():
            if leads:
                fall_copy.wait_recv()
                mate_copy.start()
                if levels > 2:

                    @pl.when(level > 0)
                    def _():
                        fall_copy.start()

                make_factor()

        def take_down(c):
            if split and leads and c == final:
                body_down.wait_recv()
                body_side.start()
            else:
                down_copy[c].wait_recv()
                send_side(c)

        def own_part(c):
            if split and leads and c == final:
                tail_down.wait_recv()
            base[c] = base[c] - product(turned_own[...], right_operand(own_in[c]))

        def beside_part(c, known):
            side_copy[c].wait_recv()
            value = base[c] - product(turned_next[...], right_operand(beside_in[c]))
            hand_down(c, value)
            if leads and known:
                store(c, value)
            else:
                base[c] = value

        for c in range(final):
            take_down(c)
            own_part(c)
            if c > 0:
                beside_part(c, False)
        spread_total()
        if leads:
            for c in range(1, final):
                store(c, base[c])
        take_down(final)
        if split and leads:
            tail_down.wait_recv()
            side_copy[0].wait_recv()
            own_last = product(turned_own[...], right_operand(own_in[final]))
            beside_first = product(turned_next[...], right_operand(beside_in[0]))
            base[final] = base[final] - own_last
            store(0, base[0] - beside_first)
        else:
            own_part(final)
            if final > 0:
                beside_part(0, True)
        beside_part(final, True)
        if not leads:
            mate_copy.wait_recv()
            make_factor()
            for c in range(chunks):
                store(c, base[c])
        all_sent(next_out, next_send)
        all_sent(own, up_send)
        if split and leads:
            all_sent(own_in.at[:, pl.ds(0, width - TAIL_ROWS // chunks)], side_send)
        else:
            all_sent(own_in, side_send)
        if leads and detour:

            @pl.when(is_relay)
            def _():
                all_sent(relayed, sums_send.at[0])

        if leads:
            rise_copy.wait_send()
            mate_copy.wait_send()
            if levels > 2:

                @pl.when(level > 0)
                def _():
                    fall_copy.wait_send()
        else:
            pair_copy.wait_send()
        await_down()

    @pl.when(jnp.logical_and(has_up, odd))
    def _():
        climb(True)

    if levels > 2:

        @pl.when(jnp.logical_and(level < levels - 2, even))
        def _():
            climb(False)


def per_device(factor_inv, update_blocks, update_rows, right_side):
    levels = lax.axis_size("level")
    subs = lax.axis_size("sub")
    width = factor_inv.shape[-1]
    columns = right_side.shape[-1]
    slots, block_rows = update_blocks.shape[2:4]
    chunks = columns // LANES
    hubs = subs // 2
    piece = pltpu.VMEM((chunks, width, LANES), jnp.float32)
    wide = pltpu.VMEM((width, 2 * width), jnp.bfloat16)
    line = pltpu.VMEM((1, columns), jnp.float32)
    chunk_sem = pltpu.SemaphoreType.DMA((chunks,))
    in_hbm = pl.BlockSpec(memory_space=pltpu.HBM)
    held = [
        pltpu.with_memory_space_constraint(array, pltpu.HBM)
        for array in (update_rows[0, 0], factor_inv[0, 0], update_blocks[0, 0], right_side[0, 0])
    ]
    value = pl.pallas_call(
        functools.partial(kernel, levels, subs),
        out_shape=jax.ShapeDtypeStruct((width, columns), jnp.float32),
        in_specs=[in_hbm] * 4,
        out_specs=pl.BlockSpec(memory_space=pltpu.VMEM),
        scratch_shapes=[
            pltpu.SMEM((slots,), jnp.int32),
            pltpu.VMEM((width, width), jnp.float32),
            pltpu.VMEM((slots, block_rows, width), jnp.float32),
            pltpu.VMEM((width, columns), jnp.float32),
            pltpu.VMEM((chunks, width, 2 * LANES), jnp.bfloat16),
            pltpu.VMEM((chunks, width, 2 * LANES), jnp.bfloat16),
        ]
        + [wide] * 9
        + [piece] * 7
        + [pltpu.VMEM((width // len(RELAYS), LANES), jnp.float32), piece]
        + [
            pltpu.VMEM((width // 2 + 8, width // 2), jnp.float32),
            pltpu.VMEM((width // 2, width // 2), jnp.float32),
            piece,
        ]
        + [line] * 4
        + [pltpu.VMEM((hubs - 1, 1, columns), jnp.float32)]
        + [line] * 2
        + [pltpu.SemaphoreType.DMA]
        + [pltpu.SemaphoreType.DMA((chunks if levels == 2 else 2 * chunks,))]
        + [pltpu.SemaphoreType.DMA]
        + [pltpu.SemaphoreType.DMA, chunk_sem] * 2
        + [pltpu.SemaphoreType.DMA((4,)), pltpu.SemaphoreType.DMA((3,))]
        + [pltpu.SemaphoreType.REGULAR]
        + [pltpu.SemaphoreType.DMA],
        compiler_params=pltpu.CompilerParams(
            collective_id=0, has_side_effects=True, vmem_limit_bytes=32 * 1024 * 1024
        ),
        name="staircase",
    )(*held)
    return value[None, None]


def solution(mesh):
    return jax.shard_map(
        per_device,
        mesh=mesh,
        in_specs=(
            P("level", "sub", None, None),
            P("level", "sub", None, None, None),
            P("level", "sub", None),
            P("level", "sub", None, None),
        ),
        out_specs=P("level", "sub", None, None),
        check_vma=False,
    )
```
